512 devices in a mesh: gx: 32 (over y_lo, z), gy: 16 (over x, y_hi, core).
Axes of the slice: x: 4, y: 4 (y_hi: 2, y_lo: 2; y = y_hi * 2 + y_lo), z: 16, core: 2. Of those that a mesh axis runs over, the one named last changes fastest.
Arguments:
- exciting: float32 [1024, 2, 20, 1536], P(('gx', 'gy')), may hold values from -6 to 6
- incident: float32 [1024, 2, 20, 1536], P(('gx', 'gy')), may hold values from -6 to 6
- pillar_type: int32 [1024, 1536], P(('gx', 'gy')), may hold values from 0 to 15
- type_matrix: float32 [16, 2, 20, 20], replicated, may hold values from -1 to 1
- near_coupling: float32 [2, 24, 20], replicated, may hold values from -1.2 to 1.2
- screening: float32 [20], replicated, may hold values from 1e-05 to 4
- coupling_gain: float32 [2, 20], replicated, may hold values from -6 to 6
Outputs:
- updated: float32 [1024, 2, 20, 1536], P(('gx', 'gy'))
The draws below stay inside these ranges and needn't reach their ends.
Inputs may be any that keep to these rules, and one draw needn't show every extreme that they name: `pillar_type`: each pillar's type is one of the 16 types.
All inputs are finite; a program needn't handle non-finite values.
Results may differ from the reference program's by a relative error of at most 0.000073.
Values sent between devices are 32-bit elements; how exact they have to be, the bound alone decides.
A program may use at most 64 MiB of HBM per device.

```python
import math
import jax
import jax.numpy as jnp
from jax import lax

NX = 1536
COEF = 20
TYPES = 16
OFFSETS = 24
NY = 1024


def plant(array, own_key, smallest, largest):
    longest = array.shape.index(max(array.shape))
    spots = []
    for shift in (0, 1):
        where = [jax.random.randint(jax.random.fold_in(own_key, axis), (), 0, length) for axis, length in enumerate(array.shape)]
        where[longest] = (where[longest] + shift) % array.shape[longest]
        spots.append(tuple(where))
    return array.at[spots[0]].set(smallest).at[spots[1]].set(largest)


def level_of(key, shape, split, least, top_value):
    gain = 1.0
    for axis_at, blocks in split:
        steps = jax.random.uniform(jax.random.fold_in(jax.random.fold_in(key, 6), axis_at), (blocks,), jnp.float32, least / len(split), top_value / len(split))
        gain = gain * jnp.repeat(jnp.exp(steps), shape[axis_at] // blocks).reshape((-1,) + (1,) * (len(shape) - 1 - axis_at))
    return gain


def gaussian(key, dims, deviation, most, shards=(), kind=jnp.bfloat16):
    drawn = jax.random.normal(key, dims, jnp.float32) * deviation
    if len(shards) > 0:
        drawn = level_of(key, dims, shards, -0.22, 0.18) * drawn
    return jnp.clip(drawn, min=-most, max=most).astype(kind)


def setup_inputs(seed: int = 0) -> dict:
    splits = jax.random.split(jax.random.key(seed), 8)
    exciting = gaussian(splits[0], (NY, 2, COEF, NX), 1.0, 6.0, ((0, 512),), jnp.float32)
    incident = gaussian(splits[1], (NY, 2, COEF, NX), 1.0, 6.0, ((0, 512),), jnp.float32)
    pillar_type = plant(jax.random.randint(splits[2], (NY, NX), 0, TYPES), jax.random.fold_in(splits[2], 1), 0, TYPES - 1).astype(jnp.int32)
    type_matrix = gaussian(splits[3], (TYPES, 2, COEF, COEF), (2 * COEF) ** -0.5, 1.0, (), jnp.float32)
    near_coupling = gaussian(splits[4], (2, OFFSETS, COEF), 0.2, 1.2, (), jnp.float32)
    screening = jnp.clip(jnp.exp(jax.random.uniform(splits[5], (COEF,), jnp.float32, math.log(9.999999747378752e-06), math.log(4.0))), 9.999999747378752e-06, 4.0)
    coupling_gain = gaussian(splits[6], (2, COEF), 1.0, 6.0, (), jnp.float32)
    return dict(exciting=exciting, incident=incident, pillar_type=pillar_type, type_matrix=type_matrix, near_coupling=near_coupling, screening=screening, coupling_gain=coupling_gain)


def shift_list():
    return [(row_step, col_step) for row_step in range(-2, 3) for col_step in range(-2, 3) if row_step != 0 or col_step != 0]

def reference(exciting, incident, pillar_type, type_matrix, near_coupling, screening, coupling_gain):
    real_part = type_matrix[:, 0]
    imag_part = type_matrix[:, 1]
    upper_rows = jnp.concatenate([real_part, -imag_part], axis=2)
    lower_rows = jnp.concatenate([imag_part, real_part], axis=2)
    blocks = jnp.concatenate([upper_rows, lower_rows], axis=1)
    fields = exciting.reshape(NY // 8, 8, 2 * COEF, NX)
    type_rows = pillar_type.reshape(NY // 8, 8, NX)

    def apply_types(operands):
        values, labels = operands
        chosen = jnp.take(blocks, labels, axis=0)
        return jnp.einsum('yxqp,ypx->yqx', chosen, values, precision=lax.Precision.HIGHEST)
    scattered = lax.map(apply_types, (fields, type_rows)).reshape(NY, 2, COEF, NX)
    complex_field = scattered[:, 0] + 1j * scattered[:, 1]
    spectrum = jnp.fft.fft2(complex_field, axes=(0, 2))
    wave_rows = jnp.arange(NY, dtype=jnp.int32).astype(jnp.float32)
    wave_cols = jnp.arange(NX, dtype=jnp.int32).astype(jnp.float32)
    eigenvalue = 4.0 * jnp.sin(math.pi * wave_rows / NY)[:, None, None] ** 2 + 4.0 * jnp.sin(math.pi * wave_cols / NX)[None, None, :] ** 2
    screen = screening[None, :, None]
    amplitude = jnp.sqrt(4.0 * math.pi * screen) / (screen + eigenvalue)
    kernel = (coupling_gain[0] + 1j * coupling_gain[1])[None, :, None] * amplitude
    far_field = jnp.fft.ifft2(spectrum * kernel, axes=(0, 2))
    coupling = near_coupling[0] + 1j * near_coupling[1]
    near_field = jnp.zeros_like(complex_field)
    for number, (row_step, col_step) in enumerate(shift_list()):
        near_field = near_field + coupling[number][None, :, None] * jnp.roll(complex_field, (-row_step, -col_step), axis=(0, 2))
    total_field = far_field + near_field
    result = incident + jnp.stack([jnp.real(total_field), jnp.imag(total_field)], axis=1)
    return result.astype(jnp.float32)
```

```python
import functools
import math

import jax
import jax.numpy as jnp
import ml_dtypes
import numpy as np
from jax import lax
from jax.experimental import pallas as pl
from jax.experimental.pallas import tpu as pltpu
from jax.sharding import PartitionSpec as P

F32 = jnp.float32
BF16 = jnp.bfloat16
OUTER = 12
LANES = 128
GROUP = 24
VMEM_LIMIT = 60 * 1024 * 1024


def tables(width_x, coef, parts, slots, used):
    sine = np.arange(LANES)
    angle = 2.0 * np.pi / width_x * (np.arange(OUTER)[:, None] * sine[None, :])
    twiddle = np.stack([np.cos(angle), -np.sin(angle)], axis=1).astype(np.float32)
    angle = 2.0 * np.pi / LANES * (sine[:, None] * sine[None, :] % LANES)
    cosine, sines = np.cos(angle), np.sin(angle)
    forward = np.block([[cosine, -sines], [sines, cosine]])
    backward = np.block([[cosine, sines], [-sines, cosine]])

    def split(matrix):
        high = matrix.astype(ml_dtypes.bfloat16)
        return np.stack([high, (matrix - high.astype(np.float64)).astype(ml_dtypes.bfloat16)])

    flat = np.arange(parts)[:, None] * used + np.arange(slots)[None, :]
    freq = (flat // coef % OUTER)[:, :, None] + OUTER * sine[None, None, :]
    angle = 2.0 * np.pi / width_x * freq
    phase = np.stack([np.cos(angle), np.sin(angle), 4.0 * np.sin(angle / 2.0) ** 2], axis=1)
    return twiddle, split(forward), split(backward), phase.astype(np.float32)


def scale(value, factor):
    real, imag = value
    wr, wi = factor
    wr = round(wr) if abs(wr - round(wr)) < 1e-12 else wr
    wi = round(wi) if abs(wi - round(wi)) < 1e-12 else wi
    if wi == 0:
        return value if wr == 1 else ((-real, -imag) if wr == -1 else (wr * real, wr * imag))
    if wr == 0:
        return (-imag, real) if wi == 1 else ((imag, -real) if wi == -1 else (-wi * imag, wi * real))
    return (wr * real - wi * imag, wr * imag + wi * real)


def plus(left, right):
    return (left[0] + right[0], left[1] + right[1])


def minus(left, right):
    return (left[0] - right[0], left[1] - right[1])


def root(number, length, sign):
    angle = sign * 2.0 * math.pi * (number % length) / length
    return (math.cos(angle), math.sin(angle))


def four_points(values, sign):
    even, odd = plus(values[0], values[2]), minus(values[0], values[2])
    other, turn = plus(values[1], values[3]), scale(minus(values[1], values[3]), (0.0, sign))
    return [plus(even, other), plus(odd, turn), minus(even, other), minus(odd, turn)]


def twelve_points(values, sign):
    inner = [four_points(values[start::3], sign) for start in range(3)]
    result = [None] * 12
    for k4 in range(4):
        first = inner[0][k4]
        second = scale(inner[1][k4], root(k4, 12, sign))
        third = scale(inner[2][k4], root(2 * k4, 12, sign))
        total = plus(second, third)
        result[k4] = plus(first, total)
        centre = (first[0] - 0.5 * total[0], first[1] - 0.5 * total[1])
        side = scale(minus(second, third), (0.0, sign * math.sqrt(3.0) / 2.0))
        result[k4 + 4] = plus(centre, side)
        result[k4 + 8] = minus(centre, side)
    return result


def dot32(rows, matrix_ref):
    high = rows.astype(BF16)
    low = (rows - high.astype(F32)).astype(BF16)
    dot = functools.partial(jnp.dot, preferred_element_type=F32)
    return dot(high, matrix_ref[0]) + (dot(low, matrix_ref[0]) + dot(high, matrix_ref[1]))


def pieces(ka, coef, used):
    start, found = 0, []
    while start < coef:
        part, slot = divmod(ka * coef + start, used)
        count = min(coef - start, used - slot)
        found.append((start, part, slot, count))
        start += count
    return found


def stage_forward(dims, exciting, kinds, types, twiddle, matrix, send, stacked, field, work):
    rows, coef, width_x, used, slots, type_count = dims
    lane = lax.broadcasted_iota(jnp.int32, types.shape, 1)
    value = types[...]
    high = value.astype(BF16).astype(F32)
    stacked[...] = jnp.where(lane < 4 * GROUP, high, value - high).astype(BF16)
    chunk = 2 * LANES

    def add_chunk(index, carry):
        row = index // (width_x // chunk)
        col = index % (width_x // chunk)
        span = pl.ds(pl.multiple_of(col * chunk, chunk), chunk)
        empty = jnp.zeros((GROUP - coef, chunk), F32)
        joined = jnp.concatenate(
            [exciting[row, 0, :, span], empty, exciting[row, 1, :, span], empty], axis=0
        )
        top = joined.astype(BF16)
        low = (joined - top.astype(F32)).astype(BF16)
        products = jnp.dot(
            stacked[...], jnp.concatenate([top, low, top], axis=0), preferred_element_type=F32
        )
        kind = kinds[pl.ds(row, 1), span]
        total = products[: 2 * GROUP]
        for number in range(1, type_count):
            part = products[2 * GROUP * number : 2 * GROUP * (number + 1)]
            total = jnp.where(kind == number, part, total)
        for half in range(2):
            for part in range(2):
                field[row, 2 * col + half, part] = total[
                    part * GROUP : (part + 1) * GROUP, half * LANES : (half + 1) * LANES
                ]
        return carry

    lax.fori_loop(0, rows * (width_x // chunk), add_chunk, 0)
    blank = jnp.zeros((1, LANES), F32)
    for row in range(rows):

        def butterfly(step, carry, row=row):
            sub = pl.ds(pl.multiple_of(step * 8, 8), 8)
            values = [(field[row, a, 0, sub], field[row, a, 1, sub]) for a in range(OUTER)]
            values = twelve_points(values, -1.0)
            for ka in range(OUTER):
                real, imag = values[ka]
                wr, wi = twiddle[ka, 0:1, :], twiddle[ka, 1:2, :]
                work[row, ka, sub, 0:LANES] = real * wr - imag * wi
                work[row, ka, sub, LANES : 2 * LANES] = real * wi + imag * wr
            return carry

        lax.fori_loop(0, GROUP // 8, butterfly, 0)
        turned = dot32(work[row].reshape(OUTER * GROUP, 2 * LANES), matrix)
        for ka in range(OUTER):
            for start, dest, slot, count in pieces(ka, coef, used):
                for part in range(2):
                    send[dest, row, part, slot : slot + count, :] = turned[
                        ka * GROUP + start : ka * GROUP + start + count,
                        part * LANES : (part + 1) * LANES,
                    ]
        for dest in range(send.shape[0]):
            for part in range(2):
                send[dest, row, part, used:slots, :] = blank


def column_picker(gy, dims):
    rows, coef, width_x, used, slots, type_count = dims
    flat = gy * used + lax.broadcasted_iota(jnp.int32, (slots, coef), 0)
    hit = flat % coef == lax.broadcasted_iota(jnp.int32, (slots, coef), 1)

    def pick(line):
        return jnp.sum(jnp.where(hit, line, 0.0), axis=1, keepdims=True)

    return pick


def decay(gy, dims, phase, screening):
    pick = column_picker(gy, dims)
    level = pick(screening[...])
    shift = level + phase[gy, 2]
    small, large = jnp.sqrt(shift), jnp.sqrt(shift + 4.0)
    loss = 2.0 * small / (small + large)
    return pick, level, small * large, loss


def repeated(loss, count):
    for _ in range(int(math.log2(count))):
        loss = loss * (2.0 - loss)
    return loss


def stage_sums(gy, dims, held, phase, screening, send):
    rows, coef, width_x, used, slots, type_count = dims
    ratio = 1.0 - decay(gy, dims, phase, screening)[3]
    parts = held.shape[0]
    zero = jnp.zeros((slots, LANES), F32)
    ahead, back = (zero, zero), (zero, zero)
    for step in range(parts * rows):
        place, row = divmod(step, rows)
        ahead = tuple(ratio * ahead[p] + held[place, row, p] for p in range(2))
        place, row = divmod(parts * rows - 1 - step, rows)
        back = tuple(ratio * back[p] + held[place, row, p] for p in range(2))
    for slot in range(slots):
        for part in range(2):
            send[2 * slot, part : part + 1, :] = ahead[part][slot : slot + 1]
            send[2 * slot + 1, part : part + 1, :] = back[part][slot : slot + 1]


def stage_scan(gx, gy, dims, got, phase, screening, send, store):
    parts = phase.shape[0]
    rows = dims[0]
    groups = got.shape[0]
    loss = repeated(decay(gy, dims, phase, screening)[3], parts * rows)
    store[...] = loss
    loss = store[pl.ds(gx // 2, 1), :]
    side = gx % 2
    ratio = 1.0 - loss
    whole = repeated(loss, groups)
    total = jnp.zeros((2, LANES), F32)
    for step in range(groups):
        total = ratio * total + got[step + side * (groups - 1 - 2 * step)]
    total = total / whole
    for step in range(groups):
        place = step + side * (groups - 1 - 2 * step)
        send[place] = total
        total = ratio * total + got[place]


def stage_solve(
    gy, dims, held, before, after, ends, phase, screening, gain, coupling, send, edge, near
):
    rows, coef, width_x, used, slots, type_count = dims
    parts = held.shape[0]
    length = parts * rows
    pick, level, width, loss = decay(gy, dims, phase, screening)
    ratio = 1.0 - loss
    amplitude = jnp.sqrt(4.0 * math.pi * level) / (width * width_x)
    gain_real = pick(gain[0:1, :]) * amplitude
    gain_imag = pick(gain[1:2, :]) * amplitude
    for slot in range(slots):
        for part in range(2):
            edge[0, part, slot : slot + 1, :] = ends[2 * slot, part : part + 1, :]
            edge[1, part, slot : slot + 1, :] = ends[2 * slot + 1, part : part + 1, :]
    c1, s1 = phase[gy, 0], phase[gy, 1]
    c2, s2 = c1 * c1 - s1 * s1, 2.0 * c1 * s1
    turns = {-2: (c2, -s2), -1: (c1, -s1), 1: (c1, s1), 2: (c2, s2)}
    number = 0
    for dy in range(-2, 3):
        real = imag = jnp.zeros((slots, LANES), F32)
        for dx in range(-2, 3):
            if dx == 0 and dy == 0:
                continue
            wr = pick(coupling[0, number : number + 1, :]) * (1.0 / width_x)
            wi = pick(coupling[1, number : number + 1, :]) * (1.0 / width_x)
            number += 1
            if dx == 0:
                real, imag = real + wr, imag + wi
            else:
                tr, ti = turns[dx]
                real, imag = real + (wr * tr - wi * ti), imag + (wr * ti + wi * tr)
        near[dy + 2, 0] = real
        near[dy + 2, 1] = imag

    def line(step, part):
        if step < 0:
            return before[(step + rows) % rows, part]
        if step >= length:
            return after[step - length, part]
        return held[step // rows, step % rows, part]

    ahead = (edge[0, 0], edge[0, 1])
    for step in range(length):
        ahead = tuple(ratio * ahead[p] + line(step, p) for p in range(2))
        for part in range(2):
            send[step // rows, step % rows, part] = ahead[part]
    back = (edge[1, 0], edge[1, 1])
    for step in range(length - 1, -1, -1):
        back = tuple(ratio * back[p] for p in range(2))
        both = tuple(send[step // rows, step % rows, p] + back[p] for p in range(2))
        back = tuple(back[p] + line(step, p) for p in range(2))
        real = gain_real * both[0] - gain_imag * both[1]
        imag = gain_real * both[1] + gain_imag * both[0]
        for dy in range(-2, 3):
            wr, wi = near[dy + 2, 0], near[dy + 2, 1]
            lr, li = line(step + dy, 0), line(step + dy, 1)
            real = real + (wr * lr - wi * li)
            imag = imag + (wr * li + wi * lr)
        send[step // rows, step % rows, 0] = real
        send[step // rows, step % rows, 1] = imag


def stage_backward(dims, got, incident, twiddle, matrix, out, work):
    rows, coef, width_x, used, slots, type_count = dims
    for row in range(rows):
        for ka in range(OUTER):
            for start, place, slot, count in pieces(ka, coef, used):
                for part in range(2):
                    work[row, ka, start : start + count, part * LANES : (part + 1) * LANES] = got[
                        place, row, part, slot : slot + count, :
                    ]
            work[row, ka, coef:GROUP, :] = jnp.zeros((GROUP - coef, 2 * LANES), F32)
        turned = dot32(work[row].reshape(OUTER * GROUP, 2 * LANES), matrix)
        work[row] = turned.reshape(OUTER, GROUP, 2 * LANES)
        for low in range(0, coef, 8):
            count = min(8, coef - low)
            values = []
            for ka in range(OUTER):
                real = work[row, ka, low : low + count, 0:LANES]
                imag = work[row, ka, low : low + count, LANES : 2 * LANES]
                wr, wi = twiddle[ka, 0:1, :], twiddle[ka, 1:2, :]
                values.append((real * wr + imag * wi, imag * wr - real * wi))
            values = twelve_points(values, 1.0)
            for a in range(OUTER):
                for part in range(2):
                    place = (row, part, slice(low, low + count), slice(a * LANES, (a + 1) * LANES))
                    out[place] = incident[place] + values[a][part]


def call(kernel, outs, scratch, *args, interpret=False):
    return pl.pallas_call(
        kernel,
        out_shape=jax.ShapeDtypeStruct(outs, F32),
        in_specs=[pl.BlockSpec(memory_space=pltpu.VMEM)] * len(args),
        out_specs=pl.BlockSpec(memory_space=pltpu.VMEM),
        scratch_shapes=scratch,
        compiler_params=pltpu.CompilerParams(vmem_limit_bytes=VMEM_LIMIT),
        interpret=interpret,
    )(*args)


def type_rows(type_matrix):
    wide = jnp.pad(type_matrix, ((0, 0), (0, 0), (0, GROUP - type_matrix.shape[2]), (0, GROUP - type_matrix.shape[3])))
    real, imag = wide[:, 0], wide[:, 1]
    top = jnp.concatenate([real, -imag] * 3, axis=2)
    low = jnp.concatenate([imag, real] * 3, axis=2)
    return jnp.concatenate([top, low], axis=1).reshape(-1, 6 * GROUP)


def body(exciting, incident, pillar_type, type_matrix, near_coupling, screening, coupling_gain):
    rows, _, coef, width_x = exciting.shape
    groups = lax.axis_size("gx")
    parts = lax.axis_size("gy")
    used = OUTER * coef // parts
    slots = groups // 2
    dims = (rows, coef, width_x, used, slots, type_matrix.shape[0])
    twiddle, forward, backward, phase = tables(width_x, coef, parts, slots, used)
    screening = screening.reshape(1, coef)
    big = (parts, rows, 2, slots, LANES)
    small = (groups, 2, LANES)

    def run_forward(e, k, t, tw, m, send, stacked, field, work):
        stage_forward(dims, e, k, t, tw, m, send, stacked, field, work)

    types = type_rows(type_matrix)
    work = pltpu.VMEM((rows, OUTER, GROUP, 2 * LANES), F32)
    spread = call(
        run_forward,
        big,
        [
            pltpu.VMEM(types.shape, BF16),
            pltpu.VMEM((rows, OUTER, 2, GROUP, LANES), F32),
            work,
        ],
        exciting,
        pillar_type,
        types,
        twiddle,
        forward,
    )
    held = lax.all_to_all(spread, "gy", split_axis=0, concat_axis=0, tiled=True)

    def run_sums(held, phase, s, send):
        stage_sums(lax.axis_index("gy"), dims, held, phase, s, send)

    sums = call(run_sums, small, [], held, phase, screening)
    got = lax.all_to_all(sums, "gx", split_axis=0, concat_axis=0, tiled=True)
    up = [(i, (i + 1) % groups) for i in range(groups)]
    down = [((i + 1) % groups, i) for i in range(groups)]
    before = lax.ppermute(held[parts - 1], "gx", up)
    after = lax.ppermute(held[0], "gx", down)

    def run_scan(got, phase, s, send, store):
        stage_scan(lax.axis_index("gx"), lax.axis_index("gy"), dims, got, phase, s, send, store)

    ends = call(run_scan, small, [pltpu.VMEM((slots, LANES), F32)], got, phase, screening)
    ends = lax.all_to_all(ends, "gx", split_axis=0, concat_axis=0, tiled=True)

    def run_solve(held, before, after, ends, phase, s, g, n, send, edge, near):
        stage_solve(
            lax.axis_index("gy"), dims, held, before, after, ends, phase, s, g, n, send, edge, near
        )

    solved = call(
        run_solve,
        big,
        [pltpu.VMEM((2, 2, slots, LANES), F32), pltpu.VMEM((5, 2, slots, LANES), F32)],
        held,
        before,
        after,
        ends,
        phase,
        screening,
        coupling_gain,
        near_coupling,
    )
    back = lax.all_to_all(solved, "gy", split_axis=0, concat_axis=0, tiled=True)

    def run_backward(b, i, tw, m, out, work):
        stage_backward(dims, b, i, tw, m, out, work)

    return call(run_backward, exciting.shape, [work], back, incident, twiddle, backward)


def solution(mesh):
    placed = (
        P(("gx", "gy"), None, None, None),
        P(("gx", "gy"), None, None, None),
        P(("gx", "gy"), None),
        P(),
        P(),
        P(),
        P(),
    )
    return jax.shard_map(
        body,
        mesh=mesh,
        in_specs=placed,
        out_specs=P(("gx", "gy"), None, None, None),
        check_vma=False,
    )
```

```python
import functools
import math

import jax
import jax.numpy as jnp
import ml_dtypes
import numpy as np
from jax import lax
from jax.experimental import pallas as pl
from jax.experimental.pallas import tpu as pltpu
from jax.sharding import PartitionSpec as P

F32 = jnp.float32
BF16 = jnp.bfloat16
OUTER = 12
LANES = 128
GROUP = 24
VMEM_LIMIT = 60 * 1024 * 1024


def tables(width_x, coef, parts, slots, used):
    sine = np.arange(LANES)
    angle = 2.0 * np.pi / width_x * (np.arange(OUTER)[:, None] * sine[None, :])
    twiddle = np.stack([np.cos(angle), -np.sin(angle)], axis=1).astype(np.float32)
    angle = 2.0 * np.pi / LANES * (sine[:, None] * sine[None, :] % LANES)
    cosine, sines = np.cos(angle), np.sin(angle)
    forward = np.block([[cosine, -sines], [sines, cosine]])
    backward = np.block([[cosine, sines], [-sines, cosine]])

    def split(matrix):
        high = matrix.astype(ml_dtypes.bfloat16)
        return np.stack([high, (matrix - high.astype(np.float64)).astype(ml_dtypes.bfloat16)])

    flat = np.arange(parts)[:, None] * used + np.arange(slots)[None, :]
    freq = (flat // coef % OUTER)[:, :, None] + OUTER * sine[None, None, :]
    angle = 2.0 * np.pi / width_x * freq
    phase = np.stack([np.cos(angle), np.sin(angle), 4.0 * np.sin(angle / 2.0) ** 2], axis=1)
    return twiddle, split(forward), split(backward), phase.astype(np.float32)


def scale(value, factor):
    real, imag = value
    wr, wi = factor
    wr = round(wr) if abs(wr - round(wr)) < 1e-12 else wr
    wi = round(wi) if abs(wi - round(wi)) < 1e-12 else wi
    if wi == 0:
        return value if wr == 1 else ((-real, -imag) if wr == -1 else (wr * real, wr * imag))
    if wr == 0:
        return (-imag, real) if wi == 1 else ((imag, -real) if wi == -1 else (-wi * imag, wi * real))
    return (wr * real - wi * imag, wr * imag + wi * real)


def plus(left, right):
    return (left[0] + right[0], left[1] + right[1])


def minus(left, right):
    return (left[0] - right[0], left[1] - right[1])


def root(number, length, sign):
    angle = sign * 2.0 * math.pi * (number % length) / length
    return (math.cos(angle), math.sin(angle))


def four_points(values, sign):
    even, odd = plus(values[0], values[2]), minus(values[0], values[2])
    other, turn = plus(values[1], values[3]), scale(minus(values[1], values[3]), (0.0, sign))
    return [plus(even, other), plus(odd, turn), minus(even, other), minus(odd, turn)]


def twelve_points(values, sign):
    inner = [four_points(values[start::3], sign) for start in range(3)]
    result = [None] * 12
    for k4 in range(4):
        first = inner[0][k4]
        second = scale(inner[1][k4], root(k4, 12, sign))
        third = scale(inner[2][k4], root(2 * k4, 12, sign))
        total = plus(second, third)
        result[k4] = plus(first, total)
        centre = (first[0] - 0.5 * total[0], first[1] - 0.5 * total[1])
        side = scale(minus(second, third), (0.0, sign * math.sqrt(3.0) / 2.0))
        result[k4 + 4] = plus(centre, side)
        result[k4 + 8] = minus(centre, side)
    return result


def dot32(rows, matrix_ref):
    high = rows.astype(BF16)
    low = (rows - high.astype(F32)).astype(BF16)
    dot = functools.partial(jnp.dot, preferred_element_type=F32)
    return dot(high, matrix_ref[0]) + (dot(low, matrix_ref[0]) + dot(high, matrix_ref[1]))


def pieces(ka, coef, used):
    start, found = 0, []
    while start < coef:
        part, slot = divmod(ka * coef + start, used)
        count = min(coef - start, used - slot)
        found.append((start, part, slot, count))
        start += count
    return found


def stack_types(type_matrix, spread, stacked, coef):
    spread[...] = jnp.zeros_like(spread)

    def place(number, carry):
        real, imag = type_matrix[number, 0], type_matrix[number, 1]
        for copy in range(3):
            low = 2 * GROUP * copy
            spread[number, 0:coef, low : low + coef] = real
            spread[number, 0:coef, low + GROUP : low + GROUP + coef] = -imag
            spread[number, GROUP : GROUP + coef, low : low + coef] = imag
            spread[number, GROUP : GROUP + coef, low + GROUP : low + GROUP + coef] = real
        return carry

    lax.fori_loop(0, spread.shape[0], place, 0)
    value = spread[...].reshape(stacked.shape)
    lane = lax.broadcasted_iota(jnp.int32, value.shape, 1)
    high = value.astype(BF16).astype(F32)
    stacked[...] = jnp.where(lane < 4 * GROUP, high, value - high).astype(BF16)


def forward_row(row, dims, exciting, kinds, twiddle, matrix, send, stacked, field, work):
    rows, coef, width_x, used, slots, type_count = dims
    chunk = 2 * LANES

    def add_chunk(col, carry):
        span = pl.ds(pl.multiple_of(col * chunk, chunk), chunk)
        empty = jnp.zeros((GROUP - coef, chunk), F32)
        joined = jnp.concatenate(
            [exciting[row, 0, :, span], empty, exciting[row, 1, :, span], empty], axis=0
        )
        top = joined.astype(BF16)
        low = (joined - top.astype(F32)).astype(BF16)
        products = jnp.dot(
            stacked[...], jnp.concatenate([top, low, top], axis=0), preferred_element_type=F32
        )
        kind = kinds[row : row + 1, span]
        total = products[: 2 * GROUP]
        for number in range(1, type_count):
            part = products[2 * GROUP * number : 2 * GROUP * (number + 1)]
            total = jnp.where(kind == number, part, total)
        for half in range(2):
            for part in range(2):
                field[2 * col + half, part] = total[
                    part * GROUP : (part + 1) * GROUP, half * LANES : (half + 1) * LANES
                ]
        return carry

    lax.fori_loop(0, width_x // chunk, add_chunk, 0)

    def butterfly(step, carry):
        sub = pl.ds(pl.multiple_of(step * 8, 8), 8)
        values = [(field[a, 0, sub], field[a, 1, sub]) for a in range(OUTER)]
        values = twelve_points(values, -1.0)
        for ka in range(OUTER):
            real, imag = values[ka]
            wr, wi = twiddle[ka, 0:1, :], twiddle[ka, 1:2, :]
            work[ka, sub, 0:LANES] = real * wr - imag * wi
            work[ka, sub, LANES : 2 * LANES] = real * wi + imag * wr
        return carry

    lax.fori_loop(0, GROUP // 8, butterfly, 0)
    turned = dot32(work[...].reshape(OUTER * GROUP, 2 * LANES), matrix)
    for ka in range(OUTER):
        for start, dest, slot, count in pieces(ka, coef, used):
            for part in range(2):
                send[dest, row, part, slot : slot + count, :] = turned[
                    ka * GROUP + start : ka * GROUP + start + count,
                    part * LANES : (part + 1) * LANES,
                ]
    blank = jnp.zeros((slots - used, LANES), F32)
    for dest in range(send.shape[0]):
        for part in range(2):
            send[dest, row, part, used:slots, :] = blank


def column_picker(gy, dims):
    rows, coef, width_x, used, slots, type_count = dims
    flat = gy * used + lax.broadcasted_iota(jnp.int32, (slots, coef), 0)
    hit = flat % coef == lax.broadcasted_iota(jnp.int32, (slots, coef), 1)

    def pick(line):
        return jnp.sum(jnp.where(hit, line, 0.0), axis=1, keepdims=True)

    return pick


def decay(gy, dims, phase, screening):
    pick = column_picker(gy, dims)
    level = pick(screening[...])
    shift = level + phase[gy, 2]
    small, large = jnp.sqrt(shift), jnp.sqrt(shift + 4.0)
    loss = 2.0 * small / (small + large)
    return pick, level, small * large, loss


def repeated(loss, count):
    for _ in range(int(math.log2(count))):
        loss = loss * (2.0 - loss)
    return loss


def stage_backward(dims, got, incident, twiddle, matrix, out, work):
    rows, coef, width_x, used, slots, type_count = dims
    for row in range(rows):
        for ka in range(OUTER):
            for start, place, slot, count in pieces(ka, coef, used):
                for part in range(2):
                    work[ka, start : start + count, part * LANES : (part + 1) * LANES] = got[
                        place, row, part, slot : slot + count, :
                    ]
            work[ka, coef:GROUP, :] = jnp.zeros((GROUP - coef, 2 * LANES), F32)
        turned = dot32(work[...].reshape(OUTER * GROUP, 2 * LANES), matrix)
        work[...] = turned.reshape(OUTER, GROUP, 2 * LANES)
        for low in range(0, coef, 8):
            count = min(8, coef - low)
            values = []
            for ka in range(OUTER):
                real = work[ka, low : low + count, 0:LANES]
                imag = work[ka, low : low + count, LANES : 2 * LANES]
                wr, wi = twiddle[ka, 0:1, :], twiddle[ka, 1:2, :]
                values.append((real * wr + imag * wi, imag * wr - real * wi))
            values = twelve_points(values, 1.0)
            for a in range(OUTER):
                for part in range(2):
                    place = (row, part, slice(low, low + count), slice(a * LANES, (a + 1) * LANES))
                    out[place] = incident[place] + values[a][part]


def fused(
    dims,
    groups,
    parts,
    exciting,
    incident,
    kinds,
    type_matrix,
    coupling,
    screening,
    gain,
    twiddle,
    forward,
    inverse,
    phase,
    out,
    spread,
    stacked,
    field,
    work,
    send,
    held,
    sums,
    got,
    reply,
    ends,
    edge,
    near,
    level,
    ahead_all,
    back_all,
    solved,
    back,
    wide_send,
    wide_recv,
    small_send,
    small_recv,
    reply_send,
    reply_recv,
    halo_send,
    halo_recv,
    last_send,
    last_recv,
):
    rows, coef, width_x, used, slots, type_count = dims
    gx, gy = lax.axis_index("gx"), lax.axis_index("gy")
    length = parts * rows

    def near_peer(step):
        return lax.rem(gy + step, parts)

    def far_peer(step):
        return lax.rem(gx + step, groups)

    def remote(source, target, first, second, device):
        return pltpu.make_async_remote_copy(
            src_ref=source,
            dst_ref=target,
            send_sem=first,
            recv_sem=second,
            device_id=device,
            device_id_type=pl.DeviceIdType.MESH,
        )

    def each(low, high, act):
        def run(step, carry):
            act(step)
            return carry

        lax.fori_loop(low, high, run, 0)

    barrier = pltpu.get_barrier_semaphore()

    def greet(device):
        pl.semaphore_signal(barrier, inc=1, device_id=device, device_id_type=pl.DeviceIdType.MESH)

    each(1, parts, lambda step: greet((gx, near_peer(step))))
    each(1, groups, lambda step: greet((far_peer(step), gy)))

    def wide(row, step):
        peer = near_peer(step)
        return remote(
            send.at[peer, row],
            held.at[1 + gy, row],
            wide_send.at[row, step],
            wide_recv.at[row, step],
            (gx, peer),
        )

    def small(step):
        peer = far_peer(step)
        return remote(
            sums.at[peer], got.at[gx], small_send.at[step], small_recv.at[step], (peer, gy)
        )

    def answer(step):
        peer = far_peer(step)
        return remote(
            reply.at[peer], ends.at[gx], reply_send.at[step], reply_recv.at[step], (peer, gy)
        )

    def last(step):
        peer = near_peer(step)
        return remote(
            solved.at[peer], back.at[gy], last_send.at[step], last_recv.at[step], (gx, peer)
        )

    up = remote(
        held.at[parts], held.at[0], halo_send.at[0], halo_recv.at[0], (far_peer(1), gy)
    )
    down = remote(
        held.at[1],
        held.at[parts + 1],
        halo_send.at[1],
        halo_recv.at[1],
        (far_peer(groups - 1), gy),
    )

    stack_types(type_matrix, spread, stacked, coef)
    for row in range(rows):
        forward_row(row, dims, exciting, kinds, twiddle, forward, send, stacked, field, work)
        if row == 0:
            pl.semaphore_wait(barrier, parts + groups - 2)
        each(1, parts, lambda step, row=row: wide(row, step).start())
        held[1 + gy, row] = send[gy, row]

    pick, screen, width, loss = decay(gy, dims, phase, screening)
    ratio = 1.0 - loss
    amplitude = jnp.sqrt(4.0 * math.pi * screen) / (width * width_x)
    level[0] = pick(gain[0:1, :]) * amplitude
    level[1] = pick(gain[1:2, :]) * amplitude
    level[2] = repeated(loss, length)
    level[3] = ratio
    c1, s1 = phase[gy, 0], phase[gy, 1]
    c2, s2 = c1 * c1 - s1 * s1, 2.0 * c1 * s1
    turns = {-2: (c2, -s2), -1: (c1, -s1), 1: (c1, s1), 2: (c2, s2)}
    number = 0
    for dy in range(-2, 3):
        real = imag = jnp.zeros((slots, LANES), F32)
        for dx in range(-2, 3):
            if dx == 0 and dy == 0:
                continue
            wr = pick(coupling[0, number : number + 1, :]) * (1.0 / width_x)
            wi = pick(coupling[1, number : number + 1, :]) * (1.0 / width_x)
            number += 1
            if dx == 0:
                real, imag = real + wr, imag + wi
            else:
                tr, ti = turns[dx]
                real, imag = real + (wr * tr - wi * ti), imag + (wr * ti + wi * tr)
        near[dy + 2, 0] = real
        near[dy + 2, 1] = imag

    for row in range(rows):
        each(1, parts, lambda step, row=row: wide(row, step).wait_recv())
    up.start()
    down.start()
    ratio = level[3]
    zero = jnp.zeros((slots, LANES), F32)
    ahead, behind = (zero, zero), (zero, zero)
    for step in range(length):
        place, row = divmod(step, rows)
        ahead = tuple(ratio * ahead[p] + held[1 + place, row, p] for p in range(2))
        place, row = divmod(length - 1 - step, rows)
        behind = tuple(ratio * behind[p] + held[1 + place, row, p] for p in range(2))
    for slot in range(slots):
        for part in range(2):
            sums[2 * slot, part : part + 1, :] = ahead[part][slot : slot + 1]
            sums[2 * slot + 1, part : part + 1, :] = behind[part][slot : slot + 1]
    each(1, groups, lambda step: small(step).start())
    got[gx] = sums[gx]

    loss = level[2, pl.ds(gx // 2, 1), :]
    side = gx % 2
    ratio = 1.0 - loss
    whole = repeated(loss, groups)
    each(1, groups, lambda step: small(step).wait_recv())
    total = jnp.zeros((2, LANES), F32)
    for step in range(groups):
        total = ratio * total + got[step + side * (groups - 1 - 2 * step)]
    total = total / whole
    for step in range(groups):
        place = step + side * (groups - 1 - 2 * step)
        reply[place] = total
        total = ratio * total + got[place]
    each(1, groups, lambda step: answer(step).start())
    ends[gx] = reply[gx]
    each(1, groups, lambda step: answer(step).wait_recv())
    up.wait_recv()
    down.wait_recv()

    for slot in range(slots):
        for part in range(2):
            edge[0, part, slot : slot + 1, :] = ends[2 * slot, part : part + 1, :]
            edge[1, part, slot : slot + 1, :] = ends[2 * slot + 1, part : part + 1, :]
    ratio = level[3]
    ahead, behind = (edge[0, 0], edge[0, 1]), (edge[1, 0], edge[1, 1])
    for step in range(length):
        place, row = divmod(step, rows)
        ahead = tuple(ratio * ahead[p] + held[1 + place, row, p] for p in range(2))
        for p in range(2):
            ahead_all[place, row, p] = ahead[p]
        place, row = divmod(length - 1 - step, rows)
        behind = tuple(ratio * behind[p] for p in range(2))
        for p in range(2):
            back_all[place, row, p] = behind[p]
        behind = tuple(behind[p] + held[1 + place, row, p] for p in range(2))

    def combine(place, target):
        gain_real, gain_imag = level[0], level[1]
        for row in range(rows):
            both = tuple(ahead_all[place, row, p] + back_all[place, row, p] for p in range(2))
            real = gain_real * both[0] - gain_imag * both[1]
            imag = gain_real * both[1] + gain_imag * both[0]
            for dy in range(-2, 3):
                jump, other = divmod(row + dy, rows)
                wr, wi = near[dy + 2, 0], near[dy + 2, 1]
                lr = held[1 + place + jump, other, 0]
                li = held[1 + place + jump, other, 1]
                real = real + (wr * lr - wi * li)
                imag = imag + (wr * li + wi * lr)
            target[place, row, 0] = real
            target[place, row, 1] = imag

    def solve(step):
        combine(near_peer(step), solved)
        last(step).start()

    each(1, parts, solve)
    combine(gy, back)
    each(1, parts, lambda step: last(step).wait_recv())
    stage_backward(dims, back, incident, twiddle, inverse, out, work)

    for row in range(rows):
        each(1, parts, lambda step, row=row: wide(row, step).wait_send())
    each(1, groups, lambda step: small(step).wait_send())
    each(1, groups, lambda step: answer(step).wait_send())
    up.wait_send()
    down.wait_send()
    each(1, parts, lambda step: last(step).wait_send())


def body(exciting, incident, pillar_type, type_matrix, near_coupling, screening, coupling_gain):
    rows, _, coef, width_x = exciting.shape
    groups = lax.axis_size("gx")
    parts = lax.axis_size("gy")
    used = OUTER * coef // parts
    slots = groups // 2
    dims = (rows, coef, width_x, used, slots, type_matrix.shape[0])
    twiddle, forward, inverse, phase = tables(width_x, coef, parts, slots, used)
    args = (
        exciting,
        incident,
        pillar_type,
        type_matrix,
        near_coupling,
        screening.reshape(1, coef),
        coupling_gain,
        twiddle,
        forward,
        inverse,
        phase,
    )
    count = type_matrix.shape[0]
    big = pltpu.VMEM((parts, rows, 2, slots, LANES), F32)
    small = pltpu.VMEM((groups, 2, LANES), F32)
    dma = pltpu.SemaphoreType.DMA
    return pl.pallas_call(
        functools.partial(fused, dims, groups, parts),
        out_shape=jax.ShapeDtypeStruct(exciting.shape, F32),
        in_specs=[pl.BlockSpec(memory_space=pltpu.VMEM)] * len(args),
        out_specs=pl.BlockSpec(memory_space=pltpu.VMEM),
        scratch_shapes=[
            pltpu.VMEM((count, 2 * GROUP, 6 * GROUP), F32),
            pltpu.VMEM((count * 2 * GROUP, 6 * GROUP), BF16),
            pltpu.VMEM((OUTER, 2, GROUP, LANES), F32),
            pltpu.VMEM((OUTER, GROUP, 2 * LANES), F32),
            big,
            pltpu.VMEM((parts + 2, rows, 2, slots, LANES), F32),
            small,
            small,
            small,
            small,
            pltpu.VMEM((2, 2, slots, LANES), F32),
            pltpu.VMEM((5, 2, slots, LANES), F32),
            pltpu.VMEM((4, slots, LANES), F32),
            big,
            big,
            big,
            big,
            dma((rows, parts)),
            dma((rows, parts)),
            dma((groups,)),
            dma((groups,)),
            dma((groups,)),
            dma((groups,)),
            dma((2,)),
            dma((2,)),
            dma((parts,)),
            dma((parts,)),
        ],
        compiler_params=pltpu.CompilerParams(
            vmem_limit_bytes=VMEM_LIMIT, collective_id=0, has_side_effects=True
        ),
    )(*args)


def solution(mesh):
    placed = (
        P(("gx", "gy"), None, None, None),
        P(("gx", "gy"), None, None, None),
        P(("gx", "gy"), None),
        P(),
        P(),
        P(),
        P(),
    )
    return jax.shard_map(
        body,
        mesh=mesh,
        in_specs=placed,
        out_specs=P(("gx", "gy"), None, None, None),
        check_vma=False,
    )
```

```python
import functools
import math

import jax
import jax.numpy as jnp
import ml_dtypes
import numpy as np
from jax import lax
from jax.experimental import pallas as pl
from jax.experimental.pallas import tpu as pltpu
from jax.sharding import PartitionSpec as P

F32 = jnp.float32
BF16 = jnp.bfloat16
OUTER = 12
LANES = 128
GROUP = 24
VMEM_LIMIT = 60 * 1024 * 1024


def tables(width_x, coef, parts, slots, used):
    sine = np.arange(LANES)
    angle = 2.0 * np.pi / width_x * (np.arange(OUTER)[:, None] * sine[None, :])
    twiddle = np.stack([np.cos(angle), -np.sin(angle)], axis=1).astype(np.float32)
    angle = 2.0 * np.pi / LANES * (sine[:, None] * sine[None, :] % LANES)
    cosine, sines = np.cos(angle), np.sin(angle)
    forward = np.block([[cosine, -sines], [sines, cosine]])
    backward = np.block([[cosine, sines], [-sines, cosine]])

    def split(matrix):
        high = matrix.astype(ml_dtypes.bfloat16)
        return np.stack([high, (matrix - high.astype(np.float64)).astype(ml_dtypes.bfloat16)])

    flat = np.arange(parts)[:, None] * used + np.arange(slots)[None, :]
    freq = (flat // coef % OUTER)[:, :, None] + OUTER * sine[None, None, :]
    angle = 2.0 * np.pi / width_x * freq
    phase = np.stack([np.cos(angle), np.sin(angle), 4.0 * np.sin(angle / 2.0) ** 2], axis=1)
    return twiddle, split(forward), split(backward), phase.astype(np.float32)


def scale(value, factor):
    real, imag = value
    wr, wi = factor
    wr = round(wr) if abs(wr - round(wr)) < 1e-12 else wr
    wi = round(wi) if abs(wi - round(wi)) < 1e-12 else wi
    if wi == 0:
        return value if wr == 1 else ((-real, -imag) if wr == -1 else (wr * real, wr * imag))
    if wr == 0:
        return (-imag, real) if wi == 1 else ((imag, -real) if wi == -1 else (-wi * imag, wi * real))
    return (wr * real - wi * imag, wr * imag + wi * real)


def plus(left, right):
    return (left[0] + right[0], left[1] + right[1])


def minus(left, right):
    return (left[0] - right[0], left[1] - right[1])


def root(number, length, sign):
    angle = sign * 2.0 * math.pi * (number % length) / length
    return (math.cos(angle), math.sin(angle))


def four_points(values, sign):
    even, odd = plus(values[0], values[2]), minus(values[0], values[2])
    other, turn = plus(values[1], values[3]), scale(minus(values[1], values[3]), (0.0, sign))
    return [plus(even, other), plus(odd, turn), minus(even, other), minus(odd, turn)]


def twelve_points(values, sign):
    inner = [four_points(values[start::3], sign) for start in range(3)]
    result = [None] * 12
    for k4 in range(4):
        first = inner[0][k4]
        second = scale(inner[1][k4], root(k4, 12, sign))
        third = scale(inner[2][k4], root(2 * k4, 12, sign))
        total = plus(second, third)
        result[k4] = plus(first, total)
        centre = (first[0] - 0.5 * total[0], first[1] - 0.5 * total[1])
        side = scale(minus(second, third), (0.0, sign * math.sqrt(3.0) / 2.0))
        result[k4 + 4] = plus(centre, side)
        result[k4 + 8] = minus(centre, side)
    return result


def dot32(rows, matrix_ref):
    high = rows.astype(BF16)
    low = (rows - high.astype(F32)).astype(BF16)
    dot = functools.partial(jnp.dot, preferred_element_type=F32)
    return dot(high, matrix_ref[0]) + (dot(low, matrix_ref[0]) + dot(high, matrix_ref[1]))


def pieces(ka, coef, used):
    start, found = 0, []
    while start < coef:
        part, slot = divmod(ka * coef + start, used)
        count = min(coef - start, used - slot)
        found.append((start, part, slot, count))
        start += count
    return found


def stack_types(type_matrix, spread, stacked, coef):
    spread[...] = jnp.zeros_like(spread)

    def place(number, carry):
        real, imag = type_matrix[number, :, 0, :], type_matrix[number, :, 1, :]
        for copy in range(3):
            low = 2 * GROUP * copy
            spread[number, 0:coef, low : low + coef] = real
            spread[number, 0:coef, low + GROUP : low + GROUP + coef] = -imag
            spread[number, GROUP : GROUP + coef, low : low + coef] = imag
            spread[number, GROUP : GROUP + coef, low + GROUP : low + GROUP + coef] = real
        return carry

    lax.fori_loop(0, spread.shape[0], place, 0)
    value = spread[...].reshape(stacked.shape)
    lane = lax.broadcasted_iota(jnp.int32, value.shape, 1)
    high = value.astype(BF16).astype(F32)
    stacked[...] = jnp.where(lane < 4 * GROUP, high, value - high).astype(BF16)


def forward_row(row, dims, exciting, kinds, twiddle, matrix, send, stacked, field, work):
    rows, coef, width_x, used, slots, type_count = dims
    chunk = 2 * LANES

    def add_chunk(col, carry):
        span = pl.ds(pl.multiple_of(col * chunk, chunk), chunk)
        empty = jnp.zeros((GROUP - coef, chunk), F32)

        joined = jnp.concatenate(
            [exciting[row, :, 0, span], empty, exciting[row, :, 1, span], empty], axis=0
        )
        top = joined.astype(BF16)
        low = (joined - top.astype(F32)).astype(BF16)
        products = jnp.dot(
            stacked[...], jnp.concatenate([top, low, top], axis=0), preferred_element_type=F32
        )
        kind = kinds[row : row + 1, span]
        total = products[: 2 * GROUP]
        for number in range(1, type_count):
            part = products[2 * GROUP * number : 2 * GROUP * (number + 1)]
            total = jnp.where(kind == number, part, total)
        for half in range(2):
            for part in range(2):
                field[2 * col + half, part] = total[
                    part * GROUP : (part + 1) * GROUP, half * LANES : (half + 1) * LANES
                ]
        return carry

    lax.fori_loop(0, width_x // chunk, add_chunk, 0)

    def butterfly(step, carry):
        sub = pl.ds(pl.multiple_of(step * 8, 8), 8)
        values = [(field[a, 0, sub], field[a, 1, sub]) for a in range(OUTER)]
        values = twelve_points(values, -1.0)
        for ka in range(OUTER):
            real, imag = values[ka]
            wr, wi = twiddle[ka, 0:1, :], twiddle[ka, 1:2, :]
            work[ka, sub, 0:LANES] = real * wr - imag * wi
            work[ka, sub, LANES : 2 * LANES] = real * wi + imag * wr
        return carry

    lax.fori_loop(0, GROUP // 8, butterfly, 0)
    turned = dot32(work[...].reshape(OUTER * GROUP, 2 * LANES), matrix)
    for ka in range(OUTER):
        for start, dest, slot, count in pieces(ka, coef, used):
            for part in range(2):
                send[dest, row, part, slot : slot + count, :] = turned[
                    ka * GROUP + start : ka * GROUP + start + count,
                    part * LANES : (part + 1) * LANES,
                ]
    blank = jnp.zeros((slots - used, LANES), F32)
    for dest in range(send.shape[0]):
        for part in range(2):
            send[dest, row, part, used:slots, :] = blank


def one_hot(gy, dims):
    rows, coef, width_x, used, slots, type_count = dims
    flat = gy * used + lax.broadcasted_iota(jnp.int32, (slots, coef), 0)
    return flat % coef == lax.broadcasted_iota(jnp.int32, (slots, coef), 1)


def column_picker(gy, dims):
    hit = one_hot(gy, dims)

    def pick(line):
        return jnp.sum(jnp.where(hit, line, 0.0), axis=1, keepdims=True)

    return pick


def decay(gy, dims, phase, screening):
    pick = column_picker(gy, dims)
    level = pick(screening[...])
    shift = level + phase[gy, 2]
    small, large = jnp.sqrt(shift), jnp.sqrt(shift + 4.0)
    loss = 2.0 * small / (small + large)
    return pick, level, small * large, loss


def repeated(loss, count):
    for _ in range(int(math.log2(count))):
        loss = loss * (2.0 - loss)
    return loss


def backward_row(row, dims, got, incident, twiddle, matrix, out, work):
    rows, coef, width_x, used, slots, type_count = dims
    for ka in range(OUTER):
        for start, place, slot, count in pieces(ka, coef, used):
            for part in range(2):
                work[ka, start : start + count, part * LANES : (part + 1) * LANES] = got[
                    place, row, part, slot : slot + count, :
                ]
        work[ka, coef:GROUP, :] = jnp.zeros((GROUP - coef, 2 * LANES), F32)
    turned = dot32(work[...].reshape(OUTER * GROUP, 2 * LANES), matrix)
    work[...] = turned.reshape(OUTER, GROUP, 2 * LANES)
    for low in range(0, coef, 8):
        count = min(8, coef - low)
        values = []
        for ka in range(OUTER):
            real = work[ka, low : low + count, 0:LANES]
            imag = work[ka, low : low + count, LANES : 2 * LANES]
            wr, wi = twiddle[ka, 0:1, :], twiddle[ka, 1:2, :]
            values.append((real * wr + imag * wi, imag * wr - real * wi))
        values = twelve_points(values, 1.0)
        for a in range(OUTER):
            for part in range(2):
                place = (row, slice(low, low + count), part, slice(a * LANES, (a + 1) * LANES))
                out[place] = incident[place] + values[a][part]


def fused(
    dims,
    groups,
    parts,
    exciting,
    incident,
    kinds,
    type_matrix,
    coupling,
    screening,
    gain,
    twiddle,
    forward,
    inverse,
    phase,
    out,
    spread,
    stacked,
    field,
    work,
    send,
    held,
    sums,
    got,
    reply,
    ends,
    edge,
    near,
    level,
    ahead_all,
    back_all,
    solved,
    back,
    wide_send,
    wide_recv,
    small_send,
    small_recv,
    reply_send,
    reply_recv,
    halo_send,
    halo_recv,
    last_send,
    last_recv,
):
    rows, coef, width_x, used, slots, type_count = dims
    gx, gy = lax.axis_index("gx"), lax.axis_index("gy")
    length = parts * rows

    def near_peer(step):
        return lax.rem(gy + step, parts)

    def far_peer(step):
        return lax.rem(gx + step, groups)

    def remote(source, target, first, second, device):
        return pltpu.make_async_remote_copy(
            src_ref=source,
            dst_ref=target,
            send_sem=first,
            recv_sem=second,
            device_id=device,
            device_id_type=pl.DeviceIdType.MESH,
        )

    def each(low, high, act):
        def run(step, carry):
            act(step)
            return carry

        lax.fori_loop(low, high, run, 0)

    barrier = pltpu.get_barrier_semaphore()

    def greet(device):
        pl.semaphore_signal(barrier, inc=1, device_id=device, device_id_type=pl.DeviceIdType.MESH)

    each(1, parts, lambda step: greet((gx, near_peer(step))))
    each(1, groups, lambda step: greet((far_peer(step), gy)))

    def wide(row, step):
        peer = near_peer(step)
        return remote(
            send.at[peer, row],
            held.at[1 + gy, row],
            wide_send.at[row, step],
            wide_recv.at[row, step],
            (gx, peer),
        )

    def small(step):
        peer = far_peer(step)
        return remote(
            sums.at[peer], got.at[gx], small_send.at[step], small_recv.at[step], (peer, gy)
        )

    def answer(step):
        peer = far_peer(step)
        return remote(
            reply.at[peer], ends.at[gx], reply_send.at[step], reply_recv.at[step], (peer, gy)
        )

    def last(row, step):
        peer = near_peer(step)
        return remote(
            solved.at[peer, row],
            back.at[gy, row],
            last_send.at[row, step],
            last_recv.at[row, step],
            (gx, peer),
        )

    up = remote(
        held.at[parts], held.at[0], halo_send.at[0], halo_recv.at[0], (far_peer(1), gy)
    )
    down = remote(
        held.at[1],
        held.at[parts + 1],
        halo_send.at[1],
        halo_recv.at[1],
        (far_peer(groups - 1), gy),
    )

    stack_types(type_matrix, spread, stacked, coef)
    for row in range(rows):
        forward_row(row, dims, exciting, kinds, twiddle, forward, send, stacked, field, work)
        if row == 0:
            pl.semaphore_wait(barrier, parts + groups - 2)
        each(1, parts, lambda step, row=row: wide(row, step).start())
        held[1 + gy, row] = send[gy, row]

    pick, screen, width, loss = decay(gy, dims, phase, screening)
    ratio = 1.0 - loss
    amplitude = jnp.sqrt(4.0 * math.pi * screen) / (width * width_x)
    level[0] = pick(gain[0:1, :]) * amplitude
    level[1] = pick(gain[1:2, :]) * amplitude
    level[2] = repeated(loss, length)
    level[3] = ratio
    c1, s1 = phase[gy, 0], phase[gy, 1]
    c2, s2 = c1 * c1 - s1 * s1, 2.0 * c1 * s1
    turns = {-2: (c2, -s2), -1: (c1, -s1), 1: (c1, s1), 2: (c2, s2)}
    chosen = [
        jnp.dot(one_hot(gy, dims).astype(F32), coupling[:, p, :], precision=lax.Precision.HIGHEST)
        * (1.0 / width_x)
        for p in range(2)
    ]
    number = 0
    for dy in range(-2, 3):
        real = imag = jnp.zeros((slots, LANES), F32)
        for dx in range(-2, 3):
            if dx == 0 and dy == 0:
                continue
            wr, wi = (chosen[p][:, number : number + 1] for p in range(2))
            number += 1
            if dx == 0:
                real, imag = real + wr, imag + wi
            else:
                tr, ti = turns[dx]
                real, imag = real + (wr * tr - wi * ti), imag + (wr * ti + wi * tr)
        near[dy + 2, 0] = real
        near[dy + 2, 1] = imag

    for row in range(rows):
        each(1, parts, lambda step, row=row: wide(row, step).wait_recv())
    up.start()
    down.start()
    ratio = level[3]
    zero = jnp.zeros((slots, LANES), F32)
    ahead, behind = (zero, zero), (zero, zero)
    for step in range(length):
        place, row = divmod(step, rows)
        ahead = tuple(ratio * ahead[p] + held[1 + place, row, p] for p in range(2))
        place, row = divmod(length - 1 - step, rows)
        behind = tuple(ratio * behind[p] + held[1 + place, row, p] for p in range(2))
    for slot in range(slots):
        for part in range(2):
            sums[2 * slot, part : part + 1, :] = ahead[part][slot : slot + 1]
            sums[2 * slot + 1, part : part + 1, :] = behind[part][slot : slot + 1]
    each(1, groups, lambda step: small(step).start())
    got[gx] = sums[gx]

    loss = level[2, pl.ds(gx // 2, 1), :]
    side = gx % 2
    ratio = 1.0 - loss
    whole = repeated(loss, groups)
    each(1, groups, lambda step: small(step).wait_recv())
    total = jnp.zeros((2, LANES), F32)
    for step in range(groups):
        total = ratio * total + got[step + side * (groups - 1 - 2 * step)]
    total = total / whole
    for step in range(groups):
        place = step + side * (groups - 1 - 2 * step)
        reply[place] = total
        total = ratio * total + got[place]
    each(1, groups, lambda step: answer(step).start())
    ends[gx] = reply[gx]
    each(1, groups, lambda step: answer(step).wait_recv())
    up.wait_recv()
    down.wait_recv()

    for slot in range(slots):
        for part in range(2):
            edge[0, part, slot : slot + 1, :] = ends[2 * slot, part : part + 1, :]
            edge[1, part, slot : slot + 1, :] = ends[2 * slot + 1, part : part + 1, :]
    ratio = level[3]
    ahead, behind = (edge[0, 0], edge[0, 1]), (edge[1, 0], edge[1, 1])
    for step in range(length):
        place, row = divmod(step, rows)
        ahead = tuple(ratio * ahead[p] + held[1 + place, row, p] for p in range(2))
        for p in range(2):
            ahead_all[place, row, p] = ahead[p]
        place, row = divmod(length - 1 - step, rows)
        behind = tuple(ratio * behind[p] for p in range(2))
        for p in range(2):
            back_all[place, row, p] = behind[p]
        behind = tuple(behind[p] + held[1 + place, row, p] for p in range(2))

    def combine(row, place, target):
        gain_real, gain_imag = level[0], level[1]
        both = tuple(ahead_all[place, row, p] + back_all[place, row, p] for p in range(2))
        real = gain_real * both[0] - gain_imag * both[1]
        imag = gain_real * both[1] + gain_imag * both[0]
        for dy in range(-2, 3):
            jump, other = divmod(row + dy, rows)
            wr, wi = near[dy + 2, 0], near[dy + 2, 1]
            lr = held[1 + place + jump, other, 0]
            li = held[1 + place + jump, other, 1]
            real = real + (wr * lr - wi * li)
            imag = imag + (wr * li + wi * lr)
        target[place, row, 0] = real
        target[place, row, 1] = imag

    for row in range(rows):

        def solve(step, row=row):
            combine(row, near_peer(step), solved)
            last(row, step).start()

        each(1, parts, solve)
        combine(row, gy, back)
    for row in range(rows):
        each(1, parts, lambda step, row=row: last(row, step).wait_recv())
        backward_row(row, dims, back, incident, twiddle, inverse, out, work)

    for row in range(rows):
        each(1, parts, lambda step, row=row: wide(row, step).wait_send())
    each(1, groups, lambda step: small(step).wait_send())
    each(1, groups, lambda step: answer(step).wait_send())
    up.wait_send()
    down.wait_send()
    for row in range(rows):
        each(1, parts, lambda step, row=row: last(row, step).wait_send())


def body(exciting, incident, pillar_type, type_matrix, near_coupling, screening, coupling_gain):
    rows, _, coef, width_x = exciting.shape
    groups = lax.axis_size("gx")
    parts = lax.axis_size("gy")
    used = OUTER * coef // parts
    slots = groups // 2
    dims = (rows, coef, width_x, used, slots, type_matrix.shape[0])
    twiddle, forward, inverse, phase = tables(width_x, coef, parts, slots, used)


    args = (
        exciting.transpose(0, 2, 1, 3),
        incident.transpose(0, 2, 1, 3),
        pillar_type,
        type_matrix.transpose(0, 2, 1, 3),
        near_coupling.transpose(2, 0, 1),
        screening.reshape(1, coef),
        coupling_gain,
        twiddle,
        forward,
        inverse,
        phase,
    )
    count = type_matrix.shape[0]
    big = pltpu.VMEM((parts, rows, 2, slots, LANES), F32)
    small = pltpu.VMEM((groups, 2, LANES), F32)
    dma = pltpu.SemaphoreType.DMA
    result = pl.pallas_call(
        functools.partial(fused, dims, groups, parts),
        out_shape=jax.ShapeDtypeStruct((rows, coef, 2, width_x), F32),
        in_specs=[pl.BlockSpec(memory_space=pltpu.VMEM)] * len(args),
        out_specs=pl.BlockSpec(memory_space=pltpu.VMEM),
        scratch_shapes=[
            pltpu.VMEM((count, 2 * GROUP, 6 * GROUP), F32),
            pltpu.VMEM((count * 2 * GROUP, 6 * GROUP), BF16),
            pltpu.VMEM((OUTER, 2, GROUP, LANES), F32),
            pltpu.VMEM((OUTER, GROUP, 2 * LANES), F32),
            big,
            pltpu.VMEM((parts + 2, rows, 2, slots, LANES), F32),
            small,
            small,
            small,
            small,
            pltpu.VMEM((2, 2, slots, LANES), F32),
            pltpu.VMEM((5, 2, slots, LANES), F32),
            pltpu.VMEM((4, slots, LANES), F32),
            big,
            big,
            big,
            big,
            dma((rows, parts)),
            dma((rows, parts)),
            dma((groups,)),
            dma((groups,)),
            dma((groups,)),
            dma((groups,)),
            dma((2,)),
            dma((2,)),
            dma((rows, parts)),
            dma((rows, parts)),
        ],
        compiler_params=pltpu.CompilerParams(
            vmem_limit_bytes=VMEM_LIMIT, collective_id=0, has_side_effects=True
        ),
    )(*args)
    return result.transpose(0, 2, 1, 3)


def solution(mesh):
    placed = (
        P(("gx", "gy"), None, None, None),
        P(("gx", "gy"), None, None, None),
        P(("gx", "gy"), None),
        P(),
        P(),
        P(),
        P(),
    )
    return jax.shard_map(
        body,
        mesh=mesh,
        in_specs=placed,
        out_specs=P(("gx", "gy"), None, None, None),
        check_vma=False,
    )
```

```python
import functools
import math

import jax
import jax.numpy as jnp
import ml_dtypes
import numpy as np
from jax import lax
from jax.experimental import pallas as pl
from jax.experimental.pallas import tpu as pltpu
from jax.sharding import PartitionSpec as P

F32 = jnp.float32
BF16 = jnp.bfloat16
OUTER = 12
LANES = 128
GROUP = 24
SUB = 8
VMEM_LIMIT = 60 * 1024 * 1024


def tables(width_x, coef, parts, slots, used):
    sine = np.arange(LANES)
    angle = 2.0 * np.pi / width_x * (np.arange(OUTER)[:, None] * sine[None, :])
    twiddle = np.stack([np.cos(angle), -np.sin(angle)], axis=1).astype(np.float32)
    angle = 2.0 * np.pi / LANES * (sine[:, None] * sine[None, :] % LANES)
    cosine, sines = np.cos(angle), np.sin(angle)
    forward = np.block([[cosine, -sines], [sines, cosine]])
    backward = np.block([[cosine, sines], [-sines, cosine]])

    def split(matrix):
        high = matrix.astype(ml_dtypes.bfloat16)
        return np.stack([high, (matrix - high.astype(np.float64)).astype(ml_dtypes.bfloat16)])

    flat = np.arange(parts)[:, None] * used + np.arange(slots)[None, :]
    freq = (flat // coef % OUTER)[:, :, None] + OUTER * sine[None, None, :]
    angle = 2.0 * np.pi / width_x * freq
    phase = np.stack([np.cos(angle), np.sin(angle), 4.0 * np.sin(angle / 2.0) ** 2], axis=1)
    return twiddle, split(forward), split(backward), phase.astype(np.float32)


def scale(value, factor):
    real, imag = value
    wr, wi = factor
    wr = round(wr) if abs(wr - round(wr)) < 1e-12 else wr
    wi = round(wi) if abs(wi - round(wi)) < 1e-12 else wi
    if wi == 0:
        return value if wr == 1 else ((-real, -imag) if wr == -1 else (wr * real, wr * imag))
    if wr == 0:
        return (-imag, real) if wi == 1 else ((imag, -real) if wi == -1 else (-wi * imag, wi * real))
    return (wr * real - wi * imag, wr * imag + wi * real)


def plus(left, right):
    return (left[0] + right[0], left[1] + right[1])


def minus(left, right):
    return (left[0] - right[0], left[1] - right[1])


def root(number, length, sign):
    angle = sign * 2.0 * math.pi * (number % length) / length
    return (math.cos(angle), math.sin(angle))


def four_points(values, sign):
    even, odd = plus(values[0], values[2]), minus(values[0], values[2])
    other, turn = plus(values[1], values[3]), scale(minus(values[1], values[3]), (0.0, sign))
    return [plus(even, other), plus(odd, turn), minus(even, other), minus(odd, turn)]


def twelve_points(values, sign):
    inner = [four_points(values[start::3], sign) for start in range(3)]
    result = [None] * 12
    for k4 in range(4):
        first = inner[0][k4]
        second = scale(inner[1][k4], root(k4, 12, sign))
        third = scale(inner[2][k4], root(2 * k4, 12, sign))
        total = plus(second, third)
        result[k4] = plus(first, total)
        centre = (first[0] - 0.5 * total[0], first[1] - 0.5 * total[1])
        side = scale(minus(second, third), (0.0, sign * math.sqrt(3.0) / 2.0))
        result[k4 + 4] = plus(centre, side)
        result[k4 + 8] = minus(centre, side)
    return result


def dot32(rows, matrix_ref):
    high = rows.astype(BF16)
    low = (rows - high.astype(F32)).astype(BF16)
    dot = functools.partial(jnp.dot, preferred_element_type=F32)
    return dot(high, matrix_ref[0]) + (dot(low, matrix_ref[0]) + dot(high, matrix_ref[1]))


def pieces(ka, coef, used):
    start, found = 0, []
    while start < coef:
        part, slot = divmod(ka * coef + start, used)
        count = min(coef - start, used - slot, SUB - slot % SUB)
        found.append((start, part, slot, count))
        start += count
    return found


def stack_types(type_matrix, spread, stacked, coef):
    spread[...] = jnp.zeros_like(spread)

    def place(number, carry):
        real, imag = type_matrix[number, :, 0, :], type_matrix[number, :, 1, :]
        for copy in range(3):
            low = 2 * GROUP * copy
            spread[number, 0:coef, low : low + coef] = real
            spread[number, 0:coef, low + GROUP : low + GROUP + coef] = -imag
            spread[number, GROUP : GROUP + coef, low : low + coef] = imag
            spread[number, GROUP : GROUP + coef, low + GROUP : low + GROUP + coef] = real
        return carry

    lax.fori_loop(0, spread.shape[0], place, 0)
    value = spread[...].reshape(stacked.shape)
    lane = lax.broadcasted_iota(jnp.int32, value.shape, 1)
    high = value.astype(BF16).astype(F32)
    stacked[...] = jnp.where(lane < 4 * GROUP, high, value - high).astype(BF16)


def forward_row(row, dims, exciting, kinds, twiddle, matrix, send, stacked, field, work):
    rows, coef, width_x, used, slots, type_count = dims
    chunk = 2 * LANES

    def add_chunk(col, carry):
        span = pl.ds(pl.multiple_of(col * chunk, chunk), chunk)
        empty = jnp.zeros((GROUP - coef, chunk), F32)

        joined = jnp.concatenate(
            [exciting[row, :, 0, span], empty, exciting[row, :, 1, span], empty], axis=0
        )
        top = joined.astype(BF16)
        low = (joined - top.astype(F32)).astype(BF16)
        products = jnp.dot(
            stacked[...], jnp.concatenate([top, low, top], axis=0), preferred_element_type=F32
        )
        kind = kinds[row : row + 1, span]
        total = products[: 2 * GROUP]
        for number in range(1, type_count):
            part = products[2 * GROUP * number : 2 * GROUP * (number + 1)]
            total = jnp.where(kind == number, part, total)
        for half in range(2):
            for part in range(2):
                field[2 * col + half, part] = total[
                    part * GROUP : (part + 1) * GROUP, half * LANES : (half + 1) * LANES
                ]
        return carry

    lax.fori_loop(0, width_x // chunk, add_chunk, 0)

    def butterfly(step, carry):
        sub = pl.ds(pl.multiple_of(step * 8, 8), 8)
        values = [(field[a, 0, sub], field[a, 1, sub]) for a in range(OUTER)]
        values = twelve_points(values, -1.0)
        for ka in range(OUTER):
            real, imag = values[ka]
            wr, wi = twiddle[ka, 0:1, :], twiddle[ka, 1:2, :]
            work[ka, sub, 0:LANES] = real * wr - imag * wi
            work[ka, sub, LANES : 2 * LANES] = real * wi + imag * wr
        return carry

    lax.fori_loop(0, GROUP // 8, butterfly, 0)
    turned = dot32(work[...].reshape(OUTER * GROUP, 2 * LANES), matrix)
    for ka in range(OUTER):
        for start, dest, slot, count in pieces(ka, coef, used):
            for part in range(2):
                send[dest, row, slot // SUB, part, slot % SUB : slot % SUB + count, :] = turned[
                    ka * GROUP + start : ka * GROUP + start + count,
                    part * LANES : (part + 1) * LANES,
                ]
    blank = jnp.zeros((slots - used, LANES), F32)
    for dest in range(send.shape[0]):
        for part in range(2):
            send[dest, row, used // SUB, part, used % SUB : SUB, :] = blank


def one_hot(gy, dims):
    rows, coef, width_x, used, slots, type_count = dims
    flat = gy * used + lax.broadcasted_iota(jnp.int32, (slots, coef), 0)
    return flat % coef == lax.broadcasted_iota(jnp.int32, (slots, coef), 1)


def column_picker(gy, dims):
    hit = one_hot(gy, dims)

    def pick(line):
        return jnp.sum(jnp.where(hit, line, 0.0), axis=1, keepdims=True)

    return pick


def decay(gy, dims, phase, screening):
    pick = column_picker(gy, dims)
    level = pick(screening[...])
    shift = level + phase[gy, 2]
    small, large = jnp.sqrt(shift), jnp.sqrt(shift + 4.0)
    loss = 2.0 * small / (small + large)
    return pick, level, small * large, loss


def repeated(loss, count):
    for _ in range(int(math.log2(count))):
        loss = loss * (2.0 - loss)
    return loss


def backward_row(row, dims, got, incident, twiddle, matrix, out, work):
    rows, coef, width_x, used, slots, type_count = dims
    for ka in range(OUTER):
        for start, place, slot, count in pieces(ka, coef, used):
            for part in range(2):
                work[ka, start : start + count, part * LANES : (part + 1) * LANES] = got[
                    place, row, slot // SUB, part, slot % SUB : slot % SUB + count, :
                ]
        work[ka, coef:GROUP, :] = jnp.zeros((GROUP - coef, 2 * LANES), F32)
    turned = dot32(work[...].reshape(OUTER * GROUP, 2 * LANES), matrix)
    work[...] = turned.reshape(OUTER, GROUP, 2 * LANES)
    for low in range(0, coef, 8):
        count = min(8, coef - low)
        values = []
        for ka in range(OUTER):
            real = work[ka, low : low + count, 0:LANES]
            imag = work[ka, low : low + count, LANES : 2 * LANES]
            wr, wi = twiddle[ka, 0:1, :], twiddle[ka, 1:2, :]
            values.append((real * wr + imag * wi, imag * wr - real * wi))
        values = twelve_points(values, 1.0)
        for a in range(OUTER):
            for part in range(2):
                place = (row, slice(low, low + count), part, slice(a * LANES, (a + 1) * LANES))
                out[place] = incident[place] + values[a][part]


def fused(
    dims,
    groups,
    parts,
    exciting,
    incident,
    kinds,
    type_matrix,
    coupling,
    screening,
    gain,
    twiddle,
    forward,
    inverse,
    phase,
    out,
    spread,
    stacked,
    field,
    work,
    send,
    held,
    sums,
    got,
    reply,
    ends,
    edge,
    near,
    level,
    ahead_all,
    back_all,
    solved,
    back,
    wide_send,
    wide_recv,
    small_send,
    small_recv,
    reply_send,
    reply_recv,
    halo_send,
    halo_recv,
    last_send,
    last_recv,
):
    rows, coef, width_x, used, slots, type_count = dims
    gx, gy = lax.axis_index("gx"), lax.axis_index("gy")
    length = parts * rows
    halves = range(slots // SUB)

    def near_peer(step):
        return lax.rem(gy + step, parts)

    def far_peer(step):
        return lax.rem(gx + step, groups)

    def remote(source, target, first, second, device):
        return pltpu.make_async_remote_copy(
            src_ref=source,
            dst_ref=target,
            send_sem=first,
            recv_sem=second,
            device_id=device,
            device_id_type=pl.DeviceIdType.MESH,
        )

    def each(low, high, act):
        def run(step, carry):
            act(step)
            return carry

        lax.fori_loop(low, high, run, 0)

    barrier = pltpu.get_barrier_semaphore()

    def greet(device):
        pl.semaphore_signal(barrier, inc=1, device_id=device, device_id_type=pl.DeviceIdType.MESH)

    each(1, parts, lambda step: greet((gx, near_peer(step))))
    each(1, groups, lambda step: greet((far_peer(step), gy)))

    def wide(row, half, step):
        peer = near_peer(step)
        return remote(
            send.at[peer, row, half],
            held.at[1 + gy, row, half],
            wide_send.at[row, half, step],
            wide_recv.at[row, half, step],
            (gx, peer),
        )

    def small(half, step):
        peer = far_peer(step)
        return remote(
            sums.at[half, peer],
            got.at[half, gx],
            small_send.at[half, step],
            small_recv.at[half, step],
            (peer, gy),
        )

    def answer(half, step):
        peer = far_peer(step)
        return remote(
            reply.at[half, peer],
            ends.at[half, gx],
            reply_send.at[half, step],
            reply_recv.at[half, step],
            (peer, gy),
        )

    def last(row, half, step):
        peer = near_peer(step)
        return remote(
            solved.at[peer, row, half],
            back.at[gy, row, half],
            last_send.at[row, half, step],
            last_recv.at[row, half, step],
            (gx, peer),
        )

    up = remote(
        held.at[parts], held.at[0], halo_send.at[0], halo_recv.at[0], (far_peer(1), gy)
    )
    down = remote(
        held.at[1],
        held.at[parts + 1],
        halo_send.at[1],
        halo_recv.at[1],
        (far_peer(groups - 1), gy),
    )

    stack_types(type_matrix, spread, stacked, coef)
    for row in range(rows):
        forward_row(row, dims, exciting, kinds, twiddle, forward, send, stacked, field, work)
        if row == 0:
            pl.semaphore_wait(barrier, parts + groups - 2)
        for half in halves:
            each(1, parts, lambda step, row=row, half=half: wide(row, half, step).start())
        held[1 + gy, row] = send[gy, row]

    pick, screen, width, loss = decay(gy, dims, phase, screening)
    ratio = 1.0 - loss
    amplitude = jnp.sqrt(4.0 * math.pi * screen) / (width * width_x)
    level[0] = pick(gain[0:1, :]) * amplitude
    level[1] = pick(gain[1:2, :]) * amplitude
    level[2] = repeated(loss, length)
    level[3] = ratio
    c1, s1 = phase[gy, 0], phase[gy, 1]
    c2, s2 = c1 * c1 - s1 * s1, 2.0 * c1 * s1
    turns = {-2: (c2, -s2), -1: (c1, -s1), 1: (c1, s1), 2: (c2, s2)}
    chosen = [
        jnp.dot(one_hot(gy, dims).astype(F32), coupling[:, p, :], precision=lax.Precision.HIGHEST)
        * (1.0 / width_x)
        for p in range(2)
    ]
    number = 0
    for dy in range(-2, 3):
        real = imag = jnp.zeros((slots, LANES), F32)
        for dx in range(-2, 3):
            if dx == 0 and dy == 0:
                continue
            wr, wi = (chosen[p][:, number : number + 1] for p in range(2))
            number += 1
            if dx == 0:
                real, imag = real + wr, imag + wi
            else:
                tr, ti = turns[dx]
                real, imag = real + (wr * tr - wi * ti), imag + (wr * ti + wi * tr)
        near[dy + 2, 0] = real
        near[dy + 2, 1] = imag

    zero = jnp.zeros((SUB, LANES), F32)
    for half in halves:
        for row in range(rows):
            each(1, parts, lambda step, row=row, half=half: wide(row, half, step).wait_recv())
        if half == halves[-1]:
            up.start()
            down.start()
        ratio = level[3, SUB * half : SUB * (half + 1), :]
        ahead, behind = (zero, zero), (zero, zero)
        for step in range(length):
            place, row = divmod(step, rows)
            ahead = tuple(ratio * ahead[p] + held[1 + place, row, half, p] for p in range(2))
            place, row = divmod(length - 1 - step, rows)
            behind = tuple(ratio * behind[p] + held[1 + place, row, half, p] for p in range(2))
        for slot in range(SUB):
            for part in range(2):
                sums[half, 4 * slot + part] = ahead[part][slot : slot + 1]
                sums[half, 4 * slot + 2 + part] = behind[part][slot : slot + 1]
        each(1, groups, lambda step, half=half: small(half, step).start())
        got[half, gx] = sums[half, gx]

    side = gx // 2 % 2
    for half in halves:
        loss = level[2, pl.ds(SUB * half + gx // 4, 1), :]
        ratio = 1.0 - loss
        whole = repeated(loss, groups)
        each(1, groups, lambda step, half=half: small(half, step).wait_recv())
        total = jnp.zeros((1, LANES), F32)
        for step in range(groups):
            total = ratio * total + got[half, step + side * (groups - 1 - 2 * step)]
        total = total / whole
        for step in range(groups):
            place = step + side * (groups - 1 - 2 * step)
            reply[half, place] = total
            total = ratio * total + got[half, place]
        each(1, groups, lambda step, half=half: answer(half, step).start())
        ends[half, gx] = reply[half, gx]

    up.wait_recv()
    down.wait_recv()

    def combine(row, half, place, target):
        span = slice(SUB * half, SUB * (half + 1))
        gain_real, gain_imag = level[0, span, :], level[1, span, :]
        both = tuple(ahead_all[place, row, p] + back_all[place, row, p] for p in range(2))
        real = gain_real * both[0] - gain_imag * both[1]
        imag = gain_real * both[1] + gain_imag * both[0]
        for dy in range(-2, 3):
            jump, other = divmod(row + dy, rows)
            wr, wi = near[dy + 2, 0, span, :], near[dy + 2, 1, span, :]
            lr = held[1 + place + jump, other, half, 0]
            li = held[1 + place + jump, other, half, 1]
            real = real + (wr * lr - wi * li)
            imag = imag + (wr * li + wi * lr)
        target[place, row, half, 0] = real
        target[place, row, half, 1] = imag

    for half in halves:
        each(1, groups, lambda step, half=half: answer(half, step).wait_recv())
        for slot in range(SUB):
            for part in range(2):
                for way in range(2):
                    edge[way, part, slot : slot + 1, :] = ends[half, 4 * slot + 2 * way + part]
        ratio = level[3, SUB * half : SUB * (half + 1), :]
        ahead, behind = (edge[0, 0], edge[0, 1]), (edge[1, 0], edge[1, 1])
        for step in range(length):
            place, row = divmod(step, rows)
            ahead = tuple(ratio * ahead[p] + held[1 + place, row, half, p] for p in range(2))
            for p in range(2):
                ahead_all[place, row, p] = ahead[p]
            place, row = divmod(length - 1 - step, rows)
            behind = tuple(ratio * behind[p] for p in range(2))
            for p in range(2):
                back_all[place, row, p] = behind[p]
            behind = tuple(behind[p] + held[1 + place, row, half, p] for p in range(2))
        for row in range(rows):

            def solve(step, row=row, half=half):
                combine(row, half, near_peer(step), solved)
                last(row, half, step).start()

            each(1, parts, solve)
            combine(row, half, gy, back)

    for row in range(rows):
        for half in halves:
            each(1, parts, lambda step, row=row, half=half: last(row, half, step).wait_recv())
        backward_row(row, dims, back, incident, twiddle, inverse, out, work)

    up.wait_send()
    down.wait_send()
    for half in halves:
        for row in range(rows):
            each(1, parts, lambda step, row=row, half=half: wide(row, half, step).wait_send())
            each(1, parts, lambda step, row=row, half=half: last(row, half, step).wait_send())
        each(1, groups, lambda step, half=half: small(half, step).wait_send())
        each(1, groups, lambda step, half=half: answer(half, step).wait_send())


def body(exciting, incident, pillar_type, type_matrix, near_coupling, screening, coupling_gain):
    rows, _, coef, width_x = exciting.shape
    groups = lax.axis_size("gx")
    parts = lax.axis_size("gy")
    used = OUTER * coef // parts
    slots = groups // 2
    dims = (rows, coef, width_x, used, slots, type_matrix.shape[0])
    twiddle, forward, inverse, phase = tables(width_x, coef, parts, slots, used)


    args = (
        exciting.transpose(0, 2, 1, 3),
        incident.transpose(0, 2, 1, 3),
        pillar_type,
        type_matrix.transpose(0, 2, 1, 3),
        near_coupling.transpose(2, 0, 1),
        screening.reshape(1, coef),
        coupling_gain,
        twiddle,
        forward,
        inverse,
        phase,
    )
    count = type_matrix.shape[0]
    halves = slots // SUB
    big = pltpu.VMEM((parts, rows, halves, 2, SUB, LANES), F32)
    line = pltpu.VMEM((parts, rows, 2, SUB, LANES), F32)
    small = pltpu.VMEM((halves, groups, 1, LANES), F32)
    dma = pltpu.SemaphoreType.DMA
    result = pl.pallas_call(
        functools.partial(fused, dims, groups, parts),
        out_shape=jax.ShapeDtypeStruct((rows, coef, 2, width_x), F32),
        in_specs=[pl.BlockSpec(memory_space=pltpu.VMEM)] * len(args),
        out_specs=pl.BlockSpec(memory_space=pltpu.VMEM),
        scratch_shapes=[
            pltpu.VMEM((count, 2 * GROUP, 6 * GROUP), F32),
            pltpu.VMEM((count * 2 * GROUP, 6 * GROUP), BF16),
            pltpu.VMEM((OUTER, 2, GROUP, LANES), F32),
            pltpu.VMEM((OUTER, GROUP, 2 * LANES), F32),
            big,
            pltpu.VMEM((parts + 2, rows, halves, 2, SUB, LANES), F32),
            small,
            small,
            small,
            small,
            pltpu.VMEM((2, 2, SUB, LANES), F32),
            pltpu.VMEM((5, 2, slots, LANES), F32),
            pltpu.VMEM((4, slots, LANES), F32),
            line,
            line,
            big,
            big,
            dma((rows, halves, parts)),
            dma((rows, halves, parts)),
            dma((halves, groups)),
            dma((halves, groups)),
            dma((halves, groups)),
            dma((halves, groups)),
            dma((2,)),
            dma((2,)),
            dma((rows, halves, parts)),
            dma((rows, halves, parts)),
        ],
        compiler_params=pltpu.CompilerParams(
            vmem_limit_bytes=VMEM_LIMIT, collective_id=0, has_side_effects=True
        ),
    )(*args)
    return result.transpose(0, 2, 1, 3)


def solution(mesh):
    placed = (
        P(("gx", "gy"), None, None, None),
        P(("gx", "gy"), None, None, None),
        P(("gx", "gy"), None),
        P(),
        P(),
        P(),
        P(),
    )
    return jax.shard_map(
        body,
        mesh=mesh,
        in_specs=placed,
        out_specs=P(("gx", "gy"), None, None, None),
        check_vma=False,
    )
```

```python
import functools
import math

import jax
import jax.numpy as jnp
import ml_dtypes
import numpy as np
from jax import lax
from jax.experimental import pallas as pl
from jax.experimental.pallas import tpu as pltpu
from jax.sharding import PartitionSpec as P

F32 = jnp.float32
BF16 = jnp.bfloat16
OUTER = 12
LANES = 128
GROUP = 24
VMEM_LIMIT = 60 * 1024 * 1024


def tables(width_x, coef, parts, slots, used):
    sine = np.arange(LANES)
    angle = 2.0 * np.pi / width_x * (np.arange(OUTER)[:, None] * sine[None, :])
    twiddle = np.stack([np.cos(angle), -np.sin(angle)], axis=1).astype(np.float32)
    angle = 2.0 * np.pi / LANES * (sine[:, None] * sine[None, :] % LANES)
    cosine, sines = np.cos(angle), np.sin(angle)
    forward = np.block([[cosine, -sines], [sines, cosine]])
    backward = np.block([[cosine, sines], [-sines, cosine]])

    def split(matrix):
        high = matrix.astype(ml_dtypes.bfloat16)
        return np.stack([high, (matrix - high.astype(np.float64)).astype(ml_dtypes.bfloat16)])

    flat = np.arange(parts)[:, None] * used + np.arange(slots)[None, :]
    freq = (flat // coef % OUTER)[:, :, None] + OUTER * sine[None, None, :]
    angle = 2.0 * np.pi / width_x * freq
    phase = np.stack([np.cos(angle), np.sin(angle), 4.0 * np.sin(angle / 2.0) ** 2], axis=1)
    return twiddle, split(forward), split(backward), phase.astype(np.float32)


def scale(value, factor):
    real, imag = value
    wr, wi = factor
    wr = round(wr) if abs(wr - round(wr)) < 1e-12 else wr
    wi = round(wi) if abs(wi - round(wi)) < 1e-12 else wi
    if wi == 0:
        return value if wr == 1 else ((-real, -imag) if wr == -1 else (wr * real, wr * imag))
    if wr == 0:
        return (-imag, real) if wi == 1 else ((imag, -real) if wi == -1 else (-wi * imag, wi * real))
    return (wr * real - wi * imag, wr * imag + wi * real)


def plus(left, right):
    return (left[0] + right[0], left[1] + right[1])


def minus(left, right):
    return (left[0] - right[0], left[1] - right[1])


def root(number, length, sign):
    angle = sign * 2.0 * math.pi * (number % length) / length
    return (math.cos(angle), math.sin(angle))


def four_points(values, sign):
    even, odd = plus(values[0], values[2]), minus(values[0], values[2])
    other, turn = plus(values[1], values[3]), scale(minus(values[1], values[3]), (0.0, sign))
    return [plus(even, other), plus(odd, turn), minus(even, other), minus(odd, turn)]


def twelve_points(values, sign):
    inner = [four_points(values[start::3], sign) for start in range(3)]
    result = [None] * 12
    for k4 in range(4):
        first = inner[0][k4]
        second = scale(inner[1][k4], root(k4, 12, sign))
        third = scale(inner[2][k4], root(2 * k4, 12, sign))
        total = plus(second, third)
        result[k4] = plus(first, total)
        centre = (first[0] - 0.5 * total[0], first[1] - 0.5 * total[1])
        side = scale(minus(second, third), (0.0, sign * math.sqrt(3.0) / 2.0))
        result[k4 + 4] = plus(centre, side)
        result[k4 + 8] = minus(centre, side)
    return result


def dot32(rows, matrix_ref):
    high = rows.astype(BF16)
    low = (rows - high.astype(F32)).astype(BF16)
    dot = functools.partial(jnp.dot, preferred_element_type=F32)
    return dot(high, matrix_ref[0]) + (dot(low, matrix_ref[0]) + dot(high, matrix_ref[1]))


def pieces(ka, coef, used):
    start, found = 0, []
    while start < coef:
        part, slot = divmod(ka * coef + start, used)
        count = min(coef - start, used - slot)
        found.append((start, part, slot, count))
        start += count
    return found


def stack_types(type_matrix, spread, stacked, coef):
    spread[...] = jnp.zeros_like(spread)

    def place(number, carry):
        real, imag = type_matrix[number, :, 0, :], type_matrix[number, :, 1, :]
        for copy in range(3):
            low = 2 * GROUP * copy
            spread[number, 0:coef, low : low + coef] = real
            spread[number, 0:coef, low + GROUP : low + GROUP + coef] = -imag
            spread[number, GROUP : GROUP + coef, low : low + coef] = imag
            spread[number, GROUP : GROUP + coef, low + GROUP : low + GROUP + coef] = real
        return carry

    lax.fori_loop(0, spread.shape[0], place, 0)
    value = spread[...].reshape(stacked.shape)
    lane = lax.broadcasted_iota(jnp.int32, value.shape, 1)
    high = value.astype(BF16).astype(F32)
    stacked[...] = jnp.where(lane < 4 * GROUP, high, value - high).astype(BF16)


def forward_row(row, dims, exciting, kinds, twiddle, matrix, send, stacked, field, work):
    rows, coef, width_x, used, slots, type_count = dims
    chunk = 2 * LANES

    def add_chunk(col, carry):
        span = pl.ds(pl.multiple_of(col * chunk, chunk), chunk)
        empty = jnp.zeros((GROUP - coef, chunk), F32)

        joined = jnp.concatenate(
            [exciting[row, :, 0, span], empty, exciting[row, :, 1, span], empty], axis=0
        )
        top = joined.astype(BF16)
        low = (joined - top.astype(F32)).astype(BF16)
        products = jnp.dot(
            stacked[...], jnp.concatenate([top, low, top], axis=0), preferred_element_type=F32
        )
        kind = kinds[row : row + 1, span]
        total = products[: 2 * GROUP]
        for number in range(1, type_count):
            part = products[2 * GROUP * number : 2 * GROUP * (number + 1)]
            total = jnp.where(kind == number, part, total)
        for half in range(2):
            for part in range(2):
                field[2 * col + half, part] = total[
                    part * GROUP : (part + 1) * GROUP, half * LANES : (half + 1) * LANES
                ]
        return carry

    lax.fori_loop(0, width_x // chunk, add_chunk, 0)

    def butterfly(step, carry):
        sub = pl.ds(pl.multiple_of(step * 8, 8), 8)
        values = [(field[a, 0, sub], field[a, 1, sub]) for a in range(OUTER)]
        values = twelve_points(values, -1.0)
        for ka in range(OUTER):
            real, imag = values[ka]
            wr, wi = twiddle[ka, 0:1, :], twiddle[ka, 1:2, :]
            work[ka, sub, 0:LANES] = real * wr - imag * wi
            work[ka, sub, LANES : 2 * LANES] = real * wi + imag * wr
        return carry

    lax.fori_loop(0, GROUP // 8, butterfly, 0)
    turned = dot32(work[...].reshape(OUTER * GROUP, 2 * LANES), matrix)
    for ka in range(OUTER):
        for start, dest, slot, count in pieces(ka, coef, used):
            for part in range(2):
                send[dest, row, part, slot : slot + count, :] = turned[
                    ka * GROUP + start : ka * GROUP + start + count,
                    part * LANES : (part + 1) * LANES,
                ]
    blank = jnp.zeros((slots - used, LANES), F32)
    for dest in range(send.shape[0]):
        for part in range(2):
            send[dest, row, part, used:slots, :] = blank


def one_hot(gy, dims):
    rows, coef, width_x, used, slots, type_count = dims
    flat = gy * used + lax.broadcasted_iota(jnp.int32, (slots, coef), 0)
    return flat % coef == lax.broadcasted_iota(jnp.int32, (slots, coef), 1)


def column_picker(gy, dims):
    hit = one_hot(gy, dims)

    def pick(line):
        return jnp.sum(jnp.where(hit, line, 0.0), axis=1, keepdims=True)

    return pick


def decay(gy, dims, phase, screening):
    pick = column_picker(gy, dims)
    level = pick(screening[...])
    shift = level + phase[gy, 2]
    small, large = jnp.sqrt(shift), jnp.sqrt(shift + 4.0)
    loss = 2.0 * small / (small + large)
    return pick, level, small * large, loss


def repeated(loss, count):
    for _ in range(int(math.log2(count))):
        loss = loss * (2.0 - loss)
    return loss


def backward_row(row, dims, got, incident, twiddle, matrix, out, work):
    rows, coef, width_x, used, slots, type_count = dims
    for ka in range(OUTER):
        for start, place, slot, count in pieces(ka, coef, used):
            for part in range(2):
                work[ka, start : start + count, part * LANES : (part + 1) * LANES] = got[
                    place, row, part, slot : slot + count, :
                ]
        work[ka, coef:GROUP, :] = jnp.zeros((GROUP - coef, 2 * LANES), F32)
    turned = dot32(work[...].reshape(OUTER * GROUP, 2 * LANES), matrix)
    work[...] = turned.reshape(OUTER, GROUP, 2 * LANES)
    for low in range(0, coef, 8):
        count = min(8, coef - low)
        values = []
        for ka in range(OUTER):
            real = work[ka, low : low + count, 0:LANES]
            imag = work[ka, low : low + count, LANES : 2 * LANES]
            wr, wi = twiddle[ka, 0:1, :], twiddle[ka, 1:2, :]
            values.append((real * wr + imag * wi, imag * wr - real * wi))
        values = twelve_points(values, 1.0)
        for a in range(OUTER):
            for part in range(2):
                place = (row, slice(low, low + count), part, slice(a * LANES, (a + 1) * LANES))
                out[place] = incident[place] + values[a][part]


def fused(
    dims,
    groups,
    parts,
    exciting,
    incident,
    kinds,
    type_matrix,
    coupling,
    screening,
    gain,
    twiddle,
    forward,
    inverse,
    phase,
    out,
    spread,
    stacked,
    field,
    work,
    send,
    held,
    sums,
    got,
    reply,
    ends,
    edge,
    near,
    level,
    ahead_all,
    back_all,
    solved,
    back,
    wide_send,
    wide_recv,
    small_send,
    small_recv,
    reply_send,
    reply_recv,
    halo_send,
    halo_recv,
    last_send,
    last_recv,
):
    rows, coef, width_x, used, slots, type_count = dims
    gx, gy = lax.axis_index("gx"), lax.axis_index("gy")
    length = parts * rows

    def near_peer(step):
        return lax.rem(gy + step, parts)

    def far_peer(step):
        return lax.rem(gx + step, groups)

    def remote(source, target, first, second, device):
        return pltpu.make_async_remote_copy(
            src_ref=source,
            dst_ref=target,
            send_sem=first,
            recv_sem=second,
            device_id=device,
            device_id_type=pl.DeviceIdType.MESH,
        )

    def each(low, high, act):
        def run(step, carry):
            act(step)
            return carry

        lax.fori_loop(low, high, run, 0)

    def settle(ref, sem):
        pltpu.make_async_copy(ref, ref, sem).wait()

    others, rest = pl.ds(0, parts - 1), pl.ds(0, groups - 1)
    barrier = pltpu.get_barrier_semaphore()

    def greet(device):
        pl.semaphore_signal(barrier, inc=1, device_id=device, device_id_type=pl.DeviceIdType.MESH)

    each(1, parts, lambda step: greet((gx, near_peer(step))))
    each(1, groups, lambda step: greet((far_peer(step), gy)))

    def wide(row, step):
        peer = near_peer(step)
        return remote(
            send.at[peer, row],
            held.at[1 + gy, row],
            wide_send.at[row],
            wide_recv.at[row],
            (gx, peer),
        )

    def small(step):
        peer = far_peer(step)
        return remote(
            sums.at[peer], got.at[gx], small_send.at[0], small_recv.at[0], (peer, gy)
        )

    def answer(step):
        peer = far_peer(step)
        return remote(
            reply.at[peer], ends.at[gx], reply_send.at[0], reply_recv.at[0], (peer, gy)
        )

    def last(row, step):
        peer = near_peer(step)
        return remote(
            solved.at[peer, row],
            back.at[gy, row],
            last_send.at[row],
            last_recv.at[row],
            (gx, peer),
        )

    up = remote(
        held.at[parts], held.at[0], halo_send.at[0], halo_recv.at[0], (far_peer(1), gy)
    )
    down = remote(
        held.at[1],
        held.at[parts + 1],
        halo_send.at[1],
        halo_recv.at[1],
        (far_peer(groups - 1), gy),
    )

    stack_types(type_matrix, spread, stacked, coef)
    for row in range(rows):
        forward_row(row, dims, exciting, kinds, twiddle, forward, send, stacked, field, work)
        if row == 0:
            pl.semaphore_wait(barrier, parts + groups - 2)
        each(1, parts, lambda step, row=row: wide(row, step).start())
        held[1 + gy, row] = send[gy, row]

    pick, screen, width, loss = decay(gy, dims, phase, screening)
    ratio = 1.0 - loss
    amplitude = jnp.sqrt(4.0 * math.pi * screen) / (width * width_x)
    level[0] = pick(gain[0:1, :]) * amplitude
    level[1] = pick(gain[1:2, :]) * amplitude
    level[2] = repeated(loss, length)
    level[3] = ratio
    c1, s1 = phase[gy, 0], phase[gy, 1]
    c2, s2 = c1 * c1 - s1 * s1, 2.0 * c1 * s1
    turns = {-2: (c2, -s2), -1: (c1, -s1), 1: (c1, s1), 2: (c2, s2)}
    chosen = [
        jnp.dot(one_hot(gy, dims).astype(F32), coupling[:, p, :], precision=lax.Precision.HIGHEST)
        * (1.0 / width_x)
        for p in range(2)
    ]
    number = 0
    for dy in range(-2, 3):
        real = imag = jnp.zeros((slots, LANES), F32)
        for dx in range(-2, 3):
            if dx == 0 and dy == 0:
                continue
            wr, wi = (chosen[p][:, number : number + 1] for p in range(2))
            number += 1
            if dx == 0:
                real, imag = real + wr, imag + wi
            else:
                tr, ti = turns[dx]
                real, imag = real + (wr * tr - wi * ti), imag + (wr * ti + wi * tr)
        near[dy + 2, 0] = real
        near[dy + 2, 1] = imag

    for row in range(rows):
        settle(held.at[others, row], wide_recv.at[row])
    up.start()
    down.start()
    ratio = level[3]
    zero = jnp.zeros((slots, LANES), F32)
    ahead, behind = (zero, zero), (zero, zero)
    for step in range(length):
        place, row = divmod(step, rows)
        ahead = tuple(ratio * ahead[p] + held[1 + place, row, p] for p in range(2))
        place, row = divmod(length - 1 - step, rows)
        behind = tuple(ratio * behind[p] + held[1 + place, row, p] for p in range(2))
    for slot in range(slots):
        for part in range(2):
            sums[2 * slot, part : part + 1, :] = ahead[part][slot : slot + 1]
            sums[2 * slot + 1, part : part + 1, :] = behind[part][slot : slot + 1]
    each(1, groups, lambda step: small(step).start())
    got[gx] = sums[gx]

    loss = level[2, pl.ds(gx // 2, 1), :]
    side = gx % 2
    ratio = 1.0 - loss
    whole = repeated(loss, groups)
    settle(got.at[rest], small_recv.at[0])
    total = jnp.zeros((2, LANES), F32)
    for step in range(groups):
        total = ratio * total + got[step + side * (groups - 1 - 2 * step)]
    total = total / whole
    for step in range(groups):
        place = step + side * (groups - 1 - 2 * step)
        reply[place] = total
        total = ratio * total + got[place]
    each(1, groups, lambda step: answer(step).start())
    ends[gx] = reply[gx]
    settle(ends.at[rest], reply_recv.at[0])
    up.wait_recv()
    down.wait_recv()

    for slot in range(slots):
        for part in range(2):
            edge[0, part, slot : slot + 1, :] = ends[2 * slot, part : part + 1, :]
            edge[1, part, slot : slot + 1, :] = ends[2 * slot + 1, part : part + 1, :]
    ratio = level[3]
    ahead, behind = (edge[0, 0], edge[0, 1]), (edge[1, 0], edge[1, 1])
    for step in range(length):
        place, row = divmod(step, rows)
        ahead = tuple(ratio * ahead[p] + held[1 + place, row, p] for p in range(2))
        for p in range(2):
            ahead_all[place, row, p] = ahead[p]
        place, row = divmod(length - 1 - step, rows)
        behind = tuple(ratio * behind[p] for p in range(2))
        for p in range(2):
            back_all[place, row, p] = behind[p]
        behind = tuple(behind[p] + held[1 + place, row, p] for p in range(2))

    def combine(row, place, target):
        gain_real, gain_imag = level[0], level[1]
        both = tuple(ahead_all[place, row, p] + back_all[place, row, p] for p in range(2))
        real = gain_real * both[0] - gain_imag * both[1]
        imag = gain_real * both[1] + gain_imag * both[0]
        for dy in range(-2, 3):
            jump, other = divmod(row + dy, rows)
            wr, wi = near[dy + 2, 0], near[dy + 2, 1]
            lr = held[1 + place + jump, other, 0]
            li = held[1 + place + jump, other, 1]
            real = real + (wr * lr - wi * li)
            imag = imag + (wr * li + wi * lr)
        target[place, row, 0] = real
        target[place, row, 1] = imag

    for row in range(rows):

        def solve(step, row=row):
            combine(row, near_peer(step), solved)
            last(row, step).start()

        each(1, parts, solve)
        combine(row, gy, back)
    for row in range(rows):
        settle(back.at[others, row], last_recv.at[row])
        backward_row(row, dims, back, incident, twiddle, inverse, out, work)

    for row in range(rows):
        settle(send.at[others, row], wide_send.at[row])
    settle(sums.at[rest], small_send.at[0])
    settle(reply.at[rest], reply_send.at[0])
    up.wait_send()
    down.wait_send()
    for row in range(rows):
        settle(solved.at[others, row], last_send.at[row])


def body(exciting, incident, pillar_type, type_matrix, near_coupling, screening, coupling_gain):
    rows, _, coef, width_x = exciting.shape
    groups = lax.axis_size("gx")
    parts = lax.axis_size("gy")
    used = OUTER * coef // parts
    slots = groups // 2
    dims = (rows, coef, width_x, used, slots, type_matrix.shape[0])
    twiddle, forward, inverse, phase = tables(width_x, coef, parts, slots, used)


    args = (
        exciting.transpose(0, 2, 1, 3),
        incident.transpose(0, 2, 1, 3),
        pillar_type,
        type_matrix.transpose(0, 2, 1, 3),
        near_coupling.transpose(2, 0, 1),
        screening.reshape(1, coef),
        coupling_gain,
        twiddle,
        forward,
        inverse,
        phase,
    )
    count = type_matrix.shape[0]
    big = pltpu.VMEM((parts, rows, 2, slots, LANES), F32)
    small = pltpu.VMEM((groups, 2, LANES), F32)
    dma = pltpu.SemaphoreType.DMA
    result = pl.pallas_call(
        functools.partial(fused, dims, groups, parts),
        out_shape=jax.ShapeDtypeStruct((rows, coef, 2, width_x), F32),
        in_specs=[pl.BlockSpec(memory_space=pltpu.VMEM)] * len(args),
        out_specs=pl.BlockSpec(memory_space=pltpu.VMEM),
        scratch_shapes=[
            pltpu.VMEM((count, 2 * GROUP, 6 * GROUP), F32),
            pltpu.VMEM((count * 2 * GROUP, 6 * GROUP), BF16),
            pltpu.VMEM((OUTER, 2, GROUP, LANES), F32),
            pltpu.VMEM((OUTER, GROUP, 2 * LANES), F32),
            big,
            pltpu.VMEM((parts + 2, rows, 2, slots, LANES), F32),
            small,
            small,
            small,
            small,
            pltpu.VMEM((2, 2, slots, LANES), F32),
            pltpu.VMEM((5, 2, slots, LANES), F32),
            pltpu.VMEM((4, slots, LANES), F32),
            big,
            big,
            big,
            big,
            dma((rows,)),
            dma((rows,)),
            dma((1,)),
            dma((1,)),
            dma((1,)),
            dma((1,)),
            dma((2,)),
            dma((2,)),
            dma((rows,)),
            dma((rows,)),
        ],
        compiler_params=pltpu.CompilerParams(
            vmem_limit_bytes=VMEM_LIMIT, collective_id=0, has_side_effects=True
        ),
    )(*args)
    return result.transpose(0, 2, 1, 3)


def solution(mesh):
    placed = (
        P(("gx", "gy"), None, None, None),
        P(("gx", "gy"), None, None, None),
        P(("gx", "gy"), None),
        P(),
        P(),
        P(),
        P(),
    )
    return jax.shard_map(
        body,
        mesh=mesh,
        in_specs=placed,
        out_specs=P(("gx", "gy"), None, None, None),
        check_vma=False,
    )
```

```python
import functools
import math

import jax
import jax.numpy as jnp
import ml_dtypes
import numpy as np
from jax import lax
from jax.experimental import pallas as pl
from jax.experimental.pallas import tpu as pltpu
from jax.sharding import PartitionSpec as P

F32 = jnp.float32
BF16 = jnp.bfloat16
OUTER = 12
LANES = 128
GROUP = 24
VMEM_LIMIT = 60 * 1024 * 1024


def tables(width_x, coef, parts, slots, used):
    sine = np.arange(LANES)
    angle = 2.0 * np.pi / width_x * (np.arange(OUTER)[:, None] * sine[None, :])
    twiddle = np.stack([np.cos(angle), -np.sin(angle)], axis=1).astype(np.float32)
    angle = 2.0 * np.pi / LANES * (sine[:, None] * sine[None, :] % LANES)
    cosine, sines = np.cos(angle), np.sin(angle)
    forward = np.block([[cosine, -sines], [sines, cosine]])
    backward = np.block([[cosine, sines], [-sines, cosine]])

    def split(matrix):
        high = matrix.astype(ml_dtypes.bfloat16)
        return np.stack([high, (matrix - high.astype(np.float64)).astype(ml_dtypes.bfloat16)])

    flat = np.arange(parts)[:, None] * used + np.arange(slots)[None, :]
    freq = (flat // coef % OUTER)[:, :, None] + OUTER * sine[None, None, :]
    angle = 2.0 * np.pi / width_x * freq
    phase = np.stack([np.cos(angle), np.sin(angle), 4.0 * np.sin(angle / 2.0) ** 2], axis=1)
    return twiddle, split(forward), split(backward), phase.astype(np.float32)


def scale(value, factor):
    real, imag = value
    wr, wi = factor
    wr = round(wr) if abs(wr - round(wr)) < 1e-12 else wr
    wi = round(wi) if abs(wi - round(wi)) < 1e-12 else wi
    if wi == 0:
        return value if wr == 1 else ((-real, -imag) if wr == -1 else (wr * real, wr * imag))
    if wr == 0:
        return (-imag, real) if wi == 1 else ((imag, -real) if wi == -1 else (-wi * imag, wi * real))
    return (wr * real - wi * imag, wr * imag + wi * real)


def plus(left, right):
    return (left[0] + right[0], left[1] + right[1])


def minus(left, right):
    return (left[0] - right[0], left[1] - right[1])


def root(number, length, sign):
    angle = sign * 2.0 * math.pi * (number % length) / length
    return (math.cos(angle), math.sin(angle))


def four_points(values, sign):
    even, odd = plus(values[0], values[2]), minus(values[0], values[2])
    other, turn = plus(values[1], values[3]), scale(minus(values[1], values[3]), (0.0, sign))
    return [plus(even, other), plus(odd, turn), minus(even, other), minus(odd, turn)]


def twelve_points(values, sign):
    inner = [four_points(values[start::3], sign) for start in range(3)]
    result = [None] * 12
    for k4 in range(4):
        first = inner[0][k4]
        second = scale(inner[1][k4], root(k4, 12, sign))
        third = scale(inner[2][k4], root(2 * k4, 12, sign))
        total = plus(second, third)
        result[k4] = plus(first, total)
        centre = (first[0] - 0.5 * total[0], first[1] - 0.5 * total[1])
        side = scale(minus(second, third), (0.0, sign * math.sqrt(3.0) / 2.0))
        result[k4 + 4] = plus(centre, side)
        result[k4 + 8] = minus(centre, side)
    return result


def dot32(rows, matrix_ref):
    high = rows.astype(BF16)
    low = (rows - high.astype(F32)).astype(BF16)
    dot = functools.partial(jnp.dot, preferred_element_type=F32)
    return dot(high, matrix_ref[0]) + (dot(low, matrix_ref[0]) + dot(high, matrix_ref[1]))


def pieces(ka, coef, used):
    start, found = 0, []
    while start < coef:
        part, slot = divmod(ka * coef + start, used)
        count = min(coef - start, used - slot)
        found.append((start, part, slot, count))
        start += count
    return found


def stack_types(type_matrix, spread, stacked, coef):
    spread[...] = jnp.zeros_like(spread)

    def place(number, carry):
        real, imag = type_matrix[number, :, 0, :], type_matrix[number, :, 1, :]
        for copy in range(3):
            low = 2 * GROUP * copy
            spread[number, 0:coef, low : low + coef] = real
            spread[number, 0:coef, low + GROUP : low + GROUP + coef] = -imag
            spread[number, GROUP : GROUP + coef, low : low + coef] = imag
            spread[number, GROUP : GROUP + coef, low + GROUP : low + GROUP + coef] = real
        return carry

    lax.fori_loop(0, spread.shape[0], place, 0)
    value = spread[...].reshape(stacked.shape)
    lane = lax.broadcasted_iota(jnp.int32, value.shape, 1)
    high = value.astype(BF16).astype(F32)
    stacked[...] = jnp.where(lane < 4 * GROUP, high, value - high).astype(BF16)


def forward_row(row, dims, exciting, kinds, twiddle, matrix, send, stacked, field, work):
    rows, coef, width_x, used, slots, type_count = dims
    chunk = 2 * LANES

    def add_chunk(col, carry):
        span = pl.ds(pl.multiple_of(col * chunk, chunk), chunk)
        empty = jnp.zeros((GROUP - coef, chunk), F32)

        joined = jnp.concatenate(
            [exciting[row, :, 0, span], empty, exciting[row, :, 1, span], empty], axis=0
        )
        top = joined.astype(BF16)
        low = (joined - top.astype(F32)).astype(BF16)
        products = jnp.dot(
            stacked[...], jnp.concatenate([top, low, top], axis=0), preferred_element_type=F32
        )
        kind = kinds[row : row + 1, span]
        total = products[: 2 * GROUP]
        for number in range(1, type_count):
            part = products[2 * GROUP * number : 2 * GROUP * (number + 1)]
            total = jnp.where(kind == number, part, total)
        for half in range(2):
            for part in range(2):
                field[2 * col + half, part] = total[
                    part * GROUP : (part + 1) * GROUP, half * LANES : (half + 1) * LANES
                ]
        return carry

    lax.fori_loop(0, width_x // chunk, add_chunk, 0)

    def butterfly(step, carry):
        sub = pl.ds(pl.multiple_of(step * 8, 8), 8)
        values = [(field[a, 0, sub], field[a, 1, sub]) for a in range(OUTER)]
        values = twelve_points(values, -1.0)
        for ka in range(OUTER):
            real, imag = values[ka]
            wr, wi = twiddle[ka, 0:1, :], twiddle[ka, 1:2, :]
            work[ka, sub, 0:LANES] = real * wr - imag * wi
            work[ka, sub, LANES : 2 * LANES] = real * wi + imag * wr
        return carry

    lax.fori_loop(0, GROUP // 8, butterfly, 0)
    turned = dot32(work[...].reshape(OUTER * GROUP, 2 * LANES), matrix)
    for ka in range(OUTER):
        for start, dest, slot, count in pieces(ka, coef, used):
            for part in range(2):
                send[dest, row, part, slot : slot + count, :] = turned[
                    ka * GROUP + start : ka * GROUP + start + count,
                    part * LANES : (part + 1) * LANES,
                ]
    blank = jnp.zeros((slots - used, LANES), F32)
    for dest in range(send.shape[0]):
        for part in range(2):
            send[dest, row, part, used:slots, :] = blank


def one_hot(gy, dims):
    rows, coef, width_x, used, slots, type_count = dims
    flat = gy * used + lax.broadcasted_iota(jnp.int32, (slots, coef), 0)
    return flat % coef == lax.broadcasted_iota(jnp.int32, (slots, coef), 1)


def column_picker(gy, dims):
    hit = one_hot(gy, dims)

    def pick(line):
        return jnp.sum(jnp.where(hit, line, 0.0), axis=1, keepdims=True)

    return pick


def decay(gy, dims, phase, screening):
    pick = column_picker(gy, dims)
    level = pick(screening[...])
    shift = level + phase[gy, 2]
    small, large = jnp.sqrt(shift), jnp.sqrt(shift + 4.0)
    loss = 2.0 * small / (small + large)
    return pick, level, small * large, loss


def repeated(loss, count):
    for _ in range(int(math.log2(count))):
        loss = loss * (2.0 - loss)
    return loss


def backward_row(row, dims, got, incident, twiddle, matrix, out, work):
    rows, coef, width_x, used, slots, type_count = dims
    for ka in range(OUTER):
        for start, place, slot, count in pieces(ka, coef, used):
            for part in range(2):
                work[ka, start : start + count, part * LANES : (part + 1) * LANES] = got[
                    place, row, part, slot : slot + count, :
                ]
        work[ka, coef:GROUP, :] = jnp.zeros((GROUP - coef, 2 * LANES), F32)
    turned = dot32(work[...].reshape(OUTER * GROUP, 2 * LANES), matrix)
    work[...] = turned.reshape(OUTER, GROUP, 2 * LANES)
    for low in range(0, coef, 8):
        count = min(8, coef - low)
        values = []
        for ka in range(OUTER):
            real = work[ka, low : low + count, 0:LANES]
            imag = work[ka, low : low + count, LANES : 2 * LANES]
            wr, wi = twiddle[ka, 0:1, :], twiddle[ka, 1:2, :]
            values.append((real * wr + imag * wi, imag * wr - real * wi))
        values = twelve_points(values, 1.0)
        for a in range(OUTER):
            for part in range(2):
                place = (row, slice(low, low + count), part, slice(a * LANES, (a + 1) * LANES))
                out[place] = incident[place] + values[a][part]


def fused(
    dims,
    groups,
    parts,
    exciting,
    incident,
    kinds,
    type_matrix,
    coupling,
    screening,
    gain,
    twiddle,
    forward,
    inverse,
    phase,
    out,
    spread,
    stacked,
    field,
    work,
    send,
    held,
    sums,
    got,
    reply,
    ends,
    edge,
    near,
    level,
    ahead_all,
    back_all,
    solved,
    back,
    wide_send,
    wide_recv,
    small_send,
    small_recv,
    reply_send,
    reply_recv,
    halo_send,
    halo_recv,
    last_send,
    last_recv,
):
    rows, coef, width_x, used, slots, type_count = dims
    gx, gy = lax.axis_index("gx"), lax.axis_index("gy")
    length = parts * rows

    def near_peer(step):
        return lax.rem(gy + step, parts)

    def far_peer(step):
        return lax.rem(gx + step, groups)

    def remote(source, target, first, second, device):
        return pltpu.make_async_remote_copy(
            src_ref=source,
            dst_ref=target,
            send_sem=first,
            recv_sem=second,
            device_id=device,
            device_id_type=pl.DeviceIdType.MESH,
        )

    def each(low, high, act):
        for step in range(low, high):
            act(step)

    def looped(low, high, act):
        stride = 3 if (high - low) % 3 == 0 else 1

        def run(index, carry):
            for offset in range(stride):
                act(low + index * stride + offset)
            return carry

        lax.fori_loop(0, (high - low) // stride, run, 0)

    def settle(ref, sem):
        pltpu.make_async_copy(ref, ref, sem).wait()

    others, rest = pl.ds(0, parts - 1), pl.ds(0, groups - 1)
    barrier = pltpu.get_barrier_semaphore()

    def greet(device):
        pl.semaphore_signal(barrier, inc=1, device_id=device, device_id_type=pl.DeviceIdType.MESH)

    each(1, parts, lambda step: greet((gx, near_peer(step))))
    each(1, groups, lambda step: greet((far_peer(step), gy)))

    def wide(row, step):
        peer = near_peer(step)
        return remote(
            send.at[peer, row],
            held.at[1 + gy, row],
            wide_send.at[row],
            wide_recv.at[row],
            (gx, peer),
        )

    def small(step):
        peer = far_peer(step)
        return remote(
            sums.at[peer], got.at[gx], small_send.at[0], small_recv.at[0], (peer, gy)
        )

    def answer(step):
        peer = far_peer(step)
        return remote(
            reply.at[peer], ends.at[gx], reply_send.at[0], reply_recv.at[0], (peer, gy)
        )

    def last(row, step):
        peer = near_peer(step)
        return remote(
            solved.at[peer, row],
            back.at[gy, row],
            last_send.at[row],
            last_recv.at[row],
            (gx, peer),
        )

    up = remote(
        held.at[parts], held.at[0], halo_send.at[0], halo_recv.at[0], (far_peer(1), gy)
    )
    down = remote(
        held.at[1],
        held.at[parts + 1],
        halo_send.at[1],
        halo_recv.at[1],
        (far_peer(groups - 1), gy),
    )

    stack_types(type_matrix, spread, stacked, coef)
    for row in range(rows):
        forward_row(row, dims, exciting, kinds, twiddle, forward, send, stacked, field, work)
        if row == 0:
            pl.semaphore_wait(barrier, parts + groups - 2)
        each(1, parts, lambda step, row=row: wide(row, step).start())
        held[1 + gy, row] = send[gy, row]

    pick, screen, width, loss = decay(gy, dims, phase, screening)
    ratio = 1.0 - loss
    amplitude = jnp.sqrt(4.0 * math.pi * screen) / (width * width_x)
    level[0] = pick(gain[0:1, :]) * amplitude
    level[1] = pick(gain[1:2, :]) * amplitude
    level[2] = repeated(loss, length)
    level[3] = ratio
    c1, s1 = phase[gy, 0], phase[gy, 1]
    c2, s2 = c1 * c1 - s1 * s1, 2.0 * c1 * s1
    turns = {-2: (c2, -s2), -1: (c1, -s1), 1: (c1, s1), 2: (c2, s2)}
    chosen = [
        jnp.dot(one_hot(gy, dims).astype(F32), coupling[:, p, :], precision=lax.Precision.HIGHEST)
        * (1.0 / width_x)
        for p in range(2)
    ]
    number = 0
    for dy in range(-2, 3):
        real = imag = jnp.zeros((slots, LANES), F32)
        for dx in range(-2, 3):
            if dx == 0 and dy == 0:
                continue
            wr, wi = (chosen[p][:, number : number + 1] for p in range(2))
            number += 1
            if dx == 0:
                real, imag = real + wr, imag + wi
            else:
                tr, ti = turns[dx]
                real, imag = real + (wr * tr - wi * ti), imag + (wr * ti + wi * tr)
        near[dy + 2, 0] = real
        near[dy + 2, 1] = imag

    for row in range(rows):
        settle(held.at[others, row], wide_recv.at[row])
    up.start()
    down.start()
    ratio = level[3]
    zero = jnp.zeros((slots, LANES), F32)
    ahead, behind = (zero, zero), (zero, zero)
    for step in range(length):
        place, row = divmod(step, rows)
        ahead = tuple(ratio * ahead[p] + held[1 + place, row, p] for p in range(2))
        place, row = divmod(length - 1 - step, rows)
        behind = tuple(ratio * behind[p] + held[1 + place, row, p] for p in range(2))
    for slot in range(slots):
        for part in range(2):
            sums[2 * slot, part : part + 1, :] = ahead[part][slot : slot + 1]
            sums[2 * slot + 1, part : part + 1, :] = behind[part][slot : slot + 1]
    each(1, groups, lambda step: small(step).start())
    got[gx] = sums[gx]

    loss = level[2, pl.ds(gx // 2, 1), :]
    side = gx % 2
    ratio = 1.0 - loss
    whole = repeated(loss, groups)
    settle(got.at[rest], small_recv.at[0])
    total = jnp.zeros((2, LANES), F32)
    for step in range(groups):
        total = ratio * total + got[step + side * (groups - 1 - 2 * step)]
    total = total / whole
    for step in range(groups):
        place = step + side * (groups - 1 - 2 * step)
        reply[place] = total
        total = ratio * total + got[place]
    each(1, groups, lambda step: answer(step).start())
    ends[gx] = reply[gx]
    settle(ends.at[rest], reply_recv.at[0])
    up.wait_recv()
    down.wait_recv()

    for slot in range(slots):
        for part in range(2):
            edge[0, part, slot : slot + 1, :] = ends[2 * slot, part : part + 1, :]
            edge[1, part, slot : slot + 1, :] = ends[2 * slot + 1, part : part + 1, :]
    ratio = level[3]
    ahead, behind = (edge[0, 0], edge[0, 1]), (edge[1, 0], edge[1, 1])
    for step in range(length):
        place, row = divmod(step, rows)
        ahead = tuple(ratio * ahead[p] + held[1 + place, row, p] for p in range(2))
        for p in range(2):
            ahead_all[place, row, p] = ahead[p]
        place, row = divmod(length - 1 - step, rows)
        behind = tuple(ratio * behind[p] for p in range(2))
        for p in range(2):
            back_all[place, row, p] = behind[p]
        behind = tuple(behind[p] + held[1 + place, row, p] for p in range(2))

    def combine(row, place, target):
        gain_real, gain_imag = level[0], level[1]
        both = tuple(ahead_all[place, row, p] + back_all[place, row, p] for p in range(2))
        real = gain_real * both[0] - gain_imag * both[1]
        imag = gain_real * both[1] + gain_imag * both[0]
        for dy in range(-2, 3):
            jump, other = divmod(row + dy, rows)
            wr, wi = near[dy + 2, 0], near[dy + 2, 1]
            lr = held[1 + place + jump, other, 0]
            li = held[1 + place + jump, other, 1]
            real = real + (wr * lr - wi * li)
            imag = imag + (wr * li + wi * lr)
        target[place, row, 0] = real
        target[place, row, 1] = imag

    for row in range(rows):

        def solve(step, row=row):
            combine(row, near_peer(step), solved)
            last(row, step).start()

        looped(1, parts, solve)
        combine(row, gy, back)
    for row in range(rows):
        settle(back.at[others, row], last_recv.at[row])
        backward_row(row, dims, back, incident, twiddle, inverse, out, work)

    for row in range(rows):
        settle(send.at[others, row], wide_send.at[row])
    settle(sums.at[rest], small_send.at[0])
    settle(reply.at[rest], reply_send.at[0])
    up.wait_send()
    down.wait_send()
    for row in range(rows):
        settle(solved.at[others, row], last_send.at[row])


def body(exciting, incident, pillar_type, type_matrix, near_coupling, screening, coupling_gain):
    rows, _, coef, width_x = exciting.shape
    groups = lax.axis_size("gx")
    parts = lax.axis_size("gy")
    used = OUTER * coef // parts
    slots = groups // 2
    dims = (rows, coef, width_x, used, slots, type_matrix.shape[0])
    twiddle, forward, inverse, phase = tables(width_x, coef, parts, slots, used)


    args = (
        exciting.transpose(0, 2, 1, 3),
        incident.transpose(0, 2, 1, 3),
        pillar_type,
        type_matrix.transpose(0, 2, 1, 3),
        near_coupling.transpose(2, 0, 1),
        screening.reshape(1, coef),
        coupling_gain,
        twiddle,
        forward,
        inverse,
        phase,
    )
    count = type_matrix.shape[0]
    big = pltpu.VMEM((parts, rows, 2, slots, LANES), F32)
    small = pltpu.VMEM((groups, 2, LANES), F32)
    dma = pltpu.SemaphoreType.DMA
    result = pl.pallas_call(
        functools.partial(fused, dims, groups, parts),
        out_shape=jax.ShapeDtypeStruct((rows, coef, 2, width_x), F32),
        in_specs=[pl.BlockSpec(memory_space=pltpu.VMEM)] * len(args),
        out_specs=pl.BlockSpec(memory_space=pltpu.VMEM),
        scratch_shapes=[
            pltpu.VMEM((count, 2 * GROUP, 6 * GROUP), F32),
            pltpu.VMEM((count * 2 * GROUP, 6 * GROUP), BF16),
            pltpu.VMEM((OUTER, 2, GROUP, LANES), F32),
            pltpu.VMEM((OUTER, GROUP, 2 * LANES), F32),
            big,
            pltpu.VMEM((parts + 2, rows, 2, slots, LANES), F32),
            small,
            small,
            small,
            small,
            pltpu.VMEM((2, 2, slots, LANES), F32),
            pltpu.VMEM((5, 2, slots, LANES), F32),
            pltpu.VMEM((4, slots, LANES), F32),
            big,
            big,
            big,
            big,
            dma((rows,)),
            dma((rows,)),
            dma((1,)),
            dma((1,)),
            dma((1,)),
            dma((1,)),
            dma((2,)),
            dma((2,)),
            dma((rows,)),
            dma((rows,)),
        ],
        compiler_params=pltpu.CompilerParams(
            vmem_limit_bytes=VMEM_LIMIT, collective_id=0, has_side_effects=True
        ),
    )(*args)
    return result.transpose(0, 2, 1, 3)


def solution(mesh):
    placed = (
        P(("gx", "gy"), None, None, None),
        P(("gx", "gy"), None, None, None),
        P(("gx", "gy"), None),
        P(),
        P(),
        P(),
        P(),
    )
    return jax.shard_map(
        body,
        mesh=mesh,
        in_specs=placed,
        out_specs=P(("gx", "gy"), None, None, None),
        check_vma=False,
    )
```

```python
import functools
import math

import jax
import jax.numpy as jnp
import ml_dtypes
import numpy as np
from jax import lax
from jax.experimental import pallas as pl
from jax.experimental.pallas import tpu as pltpu
from jax.sharding import PartitionSpec as P

F32 = jnp.float32
BF16 = jnp.bfloat16
OUTER = 12
LANES = 128
GROUP = 24
SUB = 8
VMEM_LIMIT = 60 * 1024 * 1024


def tables(width_x, coef, parts, slots, used):
    sine = np.arange(LANES)
    angle = 2.0 * np.pi / width_x * (np.arange(OUTER)[:, None] * sine[None, :])
    twiddle = np.stack([np.cos(angle), -np.sin(angle)], axis=1).astype(np.float32)
    angle = 2.0 * np.pi / LANES * (sine[:, None] * sine[None, :] % LANES)
    cosine, sines = np.cos(angle), np.sin(angle)
    forward = np.block([[cosine, -sines], [sines, cosine]])
    backward = np.block([[cosine, sines], [-sines, cosine]])

    def split(matrix):
        high = matrix.astype(ml_dtypes.bfloat16)
        return np.stack([high, (matrix - high.astype(np.float64)).astype(ml_dtypes.bfloat16)])

    flat = np.arange(parts)[:, None] * used + np.arange(slots)[None, :]
    freq = (flat // coef % OUTER)[:, :, None] + OUTER * sine[None, None, :]
    angle = 2.0 * np.pi / width_x * freq
    phase = np.stack([np.cos(angle), np.sin(angle), 4.0 * np.sin(angle / 2.0) ** 2], axis=1)
    return twiddle, split(forward), split(backward), phase.astype(np.float32)


def scale(value, factor):
    real, imag = value
    wr, wi = factor
    wr = round(wr) if abs(wr - round(wr)) < 1e-12 else wr
    wi = round(wi) if abs(wi - round(wi)) < 1e-12 else wi
    if wi == 0:
        return value if wr == 1 else ((-real, -imag) if wr == -1 else (wr * real, wr * imag))
    if wr == 0:
        return (-imag, real) if wi == 1 else ((imag, -real) if wi == -1 else (-wi * imag, wi * real))
    return (wr * real - wi * imag, wr * imag + wi * real)


def plus(left, right):
    return (left[0] + right[0], left[1] + right[1])


def minus(left, right):
    return (left[0] - right[0], left[1] - right[1])


def root(number, length, sign):
    angle = sign * 2.0 * math.pi * (number % length) / length
    return (math.cos(angle), math.sin(angle))


def four_points(values, sign):
    even, odd = plus(values[0], values[2]), minus(values[0], values[2])
    other, turn = plus(values[1], values[3]), scale(minus(values[1], values[3]), (0.0, sign))
    return [plus(even, other), plus(odd, turn), minus(even, other), minus(odd, turn)]


def twelve_points(values, sign):
    inner = [four_points(values[start::3], sign) for start in range(3)]
    result = [None] * 12
    for k4 in range(4):
        first = inner[0][k4]
        second = scale(inner[1][k4], root(k4, 12, sign))
        third = scale(inner[2][k4], root(2 * k4, 12, sign))
        total = plus(second, third)
        result[k4] = plus(first, total)
        centre = (first[0] - 0.5 * total[0], first[1] - 0.5 * total[1])
        side = scale(minus(second, third), (0.0, sign * math.sqrt(3.0) / 2.0))
        result[k4 + 4] = plus(centre, side)
        result[k4 + 8] = minus(centre, side)
    return result


def dot32(rows, matrix_ref):
    high = rows.astype(BF16)
    low = (rows - high.astype(F32)).astype(BF16)
    dot = functools.partial(jnp.dot, preferred_element_type=F32)
    return dot(high, matrix_ref[0]) + (dot(low, matrix_ref[0]) + dot(high, matrix_ref[1]))


def pieces(ka, coef, used):
    start, found = 0, []
    while start < coef:
        part, slot = divmod(ka * coef + start, used)
        count = min(coef - start, used - slot, SUB - slot % SUB)
        found.append((start, part, slot, count))
        start += count
    return found


def stack_types(type_matrix, spread, stacked, coef):
    spread[...] = jnp.zeros_like(spread)

    def place(number, carry):
        real, imag = type_matrix[number, :, 0, :], type_matrix[number, :, 1, :]
        for copy in range(3):
            low = 2 * GROUP * copy
            spread[number, 0:coef, low : low + coef] = real
            spread[number, 0:coef, low + GROUP : low + GROUP + coef] = -imag
            spread[number, GROUP : GROUP + coef, low : low + coef] = imag
            spread[number, GROUP : GROUP + coef, low + GROUP : low + GROUP + coef] = real
        return carry

    lax.fori_loop(0, spread.shape[0], place, 0)
    value = spread[...].reshape(stacked.shape)
    lane = lax.broadcasted_iota(jnp.int32, value.shape, 1)
    high = value.astype(BF16).astype(F32)
    stacked[...] = jnp.where(lane < 4 * GROUP, high, value - high).astype(BF16)


def forward_row(row, dims, exciting, kinds, twiddle, matrix, send, stacked, field, work):
    rows, coef, width_x, used, slots, type_count = dims
    chunk = 2 * LANES

    def add_chunk(col, carry):
        span = pl.ds(pl.multiple_of(col * chunk, chunk), chunk)
        empty = jnp.zeros((GROUP - coef, chunk), F32)

        joined = jnp.concatenate(
            [exciting[row, :, 0, span], empty, exciting[row, :, 1, span], empty], axis=0
        )
        top = joined.astype(BF16)
        low = (joined - top.astype(F32)).astype(BF16)
        products = jnp.dot(
            stacked[...], jnp.concatenate([top, low, top], axis=0), preferred_element_type=F32
        )
        kind = kinds[row : row + 1, span]
        total = products[: 2 * GROUP]
        for number in range(1, type_count):
            part = products[2 * GROUP * number : 2 * GROUP * (number + 1)]
            total = jnp.where(kind == number, part, total)
        for half in range(2):
            for part in range(2):
                field[2 * col + half, part] = total[
                    part * GROUP : (part + 1) * GROUP, half * LANES : (half + 1) * LANES
                ]
        return carry

    lax.fori_loop(0, width_x // chunk, add_chunk, 0)

    def butterfly(step, carry):
        sub = pl.ds(pl.multiple_of(step * 8, 8), 8)
        values = [(field[a, 0, sub], field[a, 1, sub]) for a in range(OUTER)]
        values = twelve_points(values, -1.0)
        for ka in range(OUTER):
            real, imag = values[ka]
            wr, wi = twiddle[ka, 0:1, :], twiddle[ka, 1:2, :]
            work[ka, sub, 0:LANES] = real * wr - imag * wi
            work[ka, sub, LANES : 2 * LANES] = real * wi + imag * wr
        return carry

    lax.fori_loop(0, GROUP // 8, butterfly, 0)
    turned = dot32(work[...].reshape(OUTER * GROUP, 2 * LANES), matrix)
    for ka in range(OUTER):
        for start, dest, slot, count in pieces(ka, coef, used):
            for part in range(2):
                send[dest, row, slot // SUB, part, slot % SUB : slot % SUB + count, :] = turned[
                    ka * GROUP + start : ka * GROUP + start + count,
                    part * LANES : (part + 1) * LANES,
                ]
    blank = jnp.zeros((slots - used, LANES), F32)
    for dest in range(send.shape[0]):
        for part in range(2):
            send[dest, row, used // SUB, part, used % SUB : SUB, :] = blank


def one_hot(gy, dims):
    rows, coef, width_x, used, slots, type_count = dims
    flat = gy * used + lax.broadcasted_iota(jnp.int32, (slots, coef), 0)
    return flat % coef == lax.broadcasted_iota(jnp.int32, (slots, coef), 1)


def column_picker(gy, dims):
    hit = one_hot(gy, dims)

    def pick(line):
        return jnp.sum(jnp.where(hit, line, 0.0), axis=1, keepdims=True)

    return pick


def decay(gy, dims, phase, screening):
    pick = column_picker(gy, dims)
    level = pick(screening[...])
    shift = level + phase[gy, 2]
    small, large = jnp.sqrt(shift), jnp.sqrt(shift + 4.0)
    loss = 2.0 * small / (small + large)
    return pick, level, small * large, loss


def repeated(loss, count):
    for _ in range(int(math.log2(count))):
        loss = loss * (2.0 - loss)
    return loss


def backward_row(row, dims, got, incident, twiddle, matrix, out, work):
    rows, coef, width_x, used, slots, type_count = dims
    for ka in range(OUTER):
        for start, place, slot, count in pieces(ka, coef, used):
            for part in range(2):
                work[ka, start : start + count, part * LANES : (part + 1) * LANES] = got[
                    place, row, slot // SUB, part, slot % SUB : slot % SUB + count, :
                ]
        work[ka, coef:GROUP, :] = jnp.zeros((GROUP - coef, 2 * LANES), F32)
    turned = dot32(work[...].reshape(OUTER * GROUP, 2 * LANES), matrix)
    work[...] = turned.reshape(OUTER, GROUP, 2 * LANES)
    for low in range(0, coef, 8):
        count = min(8, coef - low)
        values = []
        for ka in range(OUTER):
            real = work[ka, low : low + count, 0:LANES]
            imag = work[ka, low : low + count, LANES : 2 * LANES]
            wr, wi = twiddle[ka, 0:1, :], twiddle[ka, 1:2, :]
            values.append((real * wr + imag * wi, imag * wr - real * wi))
        values = twelve_points(values, 1.0)
        for a in range(OUTER):
            for part in range(2):
                place = (row, slice(low, low + count), part, slice(a * LANES, (a + 1) * LANES))
                out[place] = incident[place] + values[a][part]


def fused(
    dims,
    groups,
    parts,
    exciting,
    incident,
    kinds,
    type_matrix,
    coupling,
    screening,
    gain,
    twiddle,
    forward,
    inverse,
    phase,
    out,
    spread,
    stacked,
    field,
    work,
    send,
    held,
    sums,
    got,
    reply,
    ends,
    edge,
    near,
    level,
    ahead_all,
    back_all,
    solved,
    back,
    wide_send,
    wide_recv,
    small_send,
    small_recv,
    reply_send,
    reply_recv,
    halo_send,
    halo_recv,
    last_send,
    last_recv,
):
    rows, coef, width_x, used, slots, type_count = dims
    gx, gy = lax.axis_index("gx"), lax.axis_index("gy")
    length = parts * rows
    halves = range(slots // SUB)

    def near_peer(step):
        return lax.rem(gy + step, parts)

    def far_peer(step):
        return lax.rem(gx + step, groups)

    def remote(source, target, first, second, device):
        return pltpu.make_async_remote_copy(
            src_ref=source,
            dst_ref=target,
            send_sem=first,
            recv_sem=second,
            device_id=device,
            device_id_type=pl.DeviceIdType.MESH,
        )

    def each(low, high, act):
        def run(step, carry):
            act(step)
            return carry

        lax.fori_loop(low, high, run, 0)

    def settle(ref, sem):
        pltpu.make_async_copy(ref, ref, sem).wait()

    others, rest = pl.ds(0, parts - 1), pl.ds(0, groups - 1)
    barrier = pltpu.get_barrier_semaphore()

    def greet(device):
        pl.semaphore_signal(barrier, inc=1, device_id=device, device_id_type=pl.DeviceIdType.MESH)

    each(1, parts, lambda step: greet((gx, near_peer(step))))
    each(1, groups, lambda step: greet((far_peer(step), gy)))

    def wide(row, half, step):
        peer = near_peer(step)
        return remote(
            send.at[peer, row, half],
            held.at[1 + gy, row, half],
            wide_send.at[row, half],
            wide_recv.at[row, half],
            (gx, peer),
        )

    def small(half, step):
        peer = far_peer(step)
        return remote(
            sums.at[half, peer],
            got.at[half, gx],
            small_send.at[half],
            small_recv.at[half],
            (peer, gy),
        )

    def answer(half, step):
        peer = far_peer(step)
        return remote(
            reply.at[half, peer],
            ends.at[half, gx],
            reply_send.at[half],
            reply_recv.at[half],
            (peer, gy),
        )

    def last(row, half, step):
        peer = near_peer(step)
        return remote(
            solved.at[peer, row, half],
            back.at[gy, row, half],
            last_send.at[row, half],
            last_recv.at[row, half],
            (gx, peer),
        )

    up = remote(
        held.at[parts], held.at[0], halo_send.at[0], halo_recv.at[0], (far_peer(1), gy)
    )
    down = remote(
        held.at[1],
        held.at[parts + 1],
        halo_send.at[1],
        halo_recv.at[1],
        (far_peer(groups - 1), gy),
    )

    stack_types(type_matrix, spread, stacked, coef)
    for row in range(rows):
        forward_row(row, dims, exciting, kinds, twiddle, forward, send, stacked, field, work)
        if row == 0:
            pl.semaphore_wait(barrier, parts + groups - 2)
        for half in halves:
            each(1, parts, lambda step, row=row, half=half: wide(row, half, step).start())
        held[1 + gy, row] = send[gy, row]

    pick, screen, width, loss = decay(gy, dims, phase, screening)
    ratio = 1.0 - loss
    amplitude = jnp.sqrt(4.0 * math.pi * screen) / (width * width_x)
    level[0] = pick(gain[0:1, :]) * amplitude
    level[1] = pick(gain[1:2, :]) * amplitude
    level[2] = repeated(loss, length)
    level[3] = ratio
    c1, s1 = phase[gy, 0], phase[gy, 1]
    c2, s2 = c1 * c1 - s1 * s1, 2.0 * c1 * s1
    turns = {-2: (c2, -s2), -1: (c1, -s1), 1: (c1, s1), 2: (c2, s2)}
    chosen = [
        jnp.dot(one_hot(gy, dims).astype(F32), coupling[:, p, :], precision=lax.Precision.HIGHEST)
        * (1.0 / width_x)
        for p in range(2)
    ]
    number = 0
    for dy in range(-2, 3):
        real = imag = jnp.zeros((slots, LANES), F32)
        for dx in range(-2, 3):
            if dx == 0 and dy == 0:
                continue
            wr, wi = (chosen[p][:, number : number + 1] for p in range(2))
            number += 1
            if dx == 0:
                real, imag = real + wr, imag + wi
            else:
                tr, ti = turns[dx]
                real, imag = real + (wr * tr - wi * ti), imag + (wr * ti + wi * tr)
        near[dy + 2, 0] = real
        near[dy + 2, 1] = imag

    zero = jnp.zeros((SUB, LANES), F32)
    for half in halves:
        for row in range(rows):
            settle(held.at[others, row, half], wide_recv.at[row, half])
        if half == halves[-1]:
            up.start()
            down.start()
        ratio = level[3, SUB * half : SUB * (half + 1), :]
        ahead, behind = (zero, zero), (zero, zero)
        for step in range(length):
            place, row = divmod(step, rows)
            ahead = tuple(ratio * ahead[p] + held[1 + place, row, half, p] for p in range(2))
            place, row = divmod(length - 1 - step, rows)
            behind = tuple(ratio * behind[p] + held[1 + place, row, half, p] for p in range(2))
        for slot in range(SUB):
            for part in range(2):
                sums[half, 4 * slot + part] = ahead[part][slot : slot + 1]
                sums[half, 4 * slot + 2 + part] = behind[part][slot : slot + 1]
        each(1, groups, lambda step, half=half: small(half, step).start())
        got[half, gx] = sums[half, gx]

    side = gx // 2 % 2
    for half in halves:
        loss = level[2, pl.ds(SUB * half + gx // 4, 1), :]
        ratio = 1.0 - loss
        whole = repeated(loss, groups)
        settle(got.at[half, rest], small_recv.at[half])
        total = jnp.zeros((1, LANES), F32)
        for step in range(groups):
            total = ratio * total + got[half, step + side * (groups - 1 - 2 * step)]
        total = total / whole
        for step in range(groups):
            place = step + side * (groups - 1 - 2 * step)
            reply[half, place] = total
            total = ratio * total + got[half, place]
        each(1, groups, lambda step, half=half: answer(half, step).start())
        ends[half, gx] = reply[half, gx]

    up.wait_recv()
    down.wait_recv()

    def combine(row, half, place, target):
        span = slice(SUB * half, SUB * (half + 1))
        gain_real, gain_imag = level[0, span, :], level[1, span, :]
        both = tuple(ahead_all[place, row, p] + back_all[place, row, p] for p in range(2))
        real = gain_real * both[0] - gain_imag * both[1]
        imag = gain_real * both[1] + gain_imag * both[0]
        for dy in range(-2, 3):
            jump, other = divmod(row + dy, rows)
            wr, wi = near[dy + 2, 0, span, :], near[dy + 2, 1, span, :]
            lr = held[1 + place + jump, other, half, 0]
            li = held[1 + place + jump, other, half, 1]
            real = real + (wr * lr - wi * li)
            imag = imag + (wr * li + wi * lr)
        target[place, row, half, 0] = real
        target[place, row, half, 1] = imag

    for half in halves:
        settle(ends.at[half, rest], reply_recv.at[half])
        for slot in range(SUB):
            for part in range(2):
                for way in range(2):
                    edge[way, part, slot : slot + 1, :] = ends[half, 4 * slot + 2 * way + part]
        ratio = level[3, SUB * half : SUB * (half + 1), :]
        ahead, behind = (edge[0, 0], edge[0, 1]), (edge[1, 0], edge[1, 1])
        for step in range(length):
            place, row = divmod(step, rows)
            ahead = tuple(ratio * ahead[p] + held[1 + place, row, half, p] for p in range(2))
            for p in range(2):
                ahead_all[place, row, p] = ahead[p]
            place, row = divmod(length - 1 - step, rows)
            behind = tuple(ratio * behind[p] for p in range(2))
            for p in range(2):
                back_all[place, row, p] = behind[p]
            behind = tuple(behind[p] + held[1 + place, row, half, p] for p in range(2))
        for row in range(rows):

            def solve(step, row=row, half=half):
                combine(row, half, near_peer(step), solved)
                last(row, half, step).start()

            each(1, parts, solve)
            combine(row, half, gy, back)

    for row in range(rows):
        for half in halves:
            settle(back.at[others, row, half], last_recv.at[row, half])
        backward_row(row, dims, back, incident, twiddle, inverse, out, work)

    up.wait_send()
    down.wait_send()
    for half in halves:
        for row in range(rows):
            settle(send.at[others, row, half], wide_send.at[row, half])
            settle(solved.at[others, row, half], last_send.at[row, half])
        settle(sums.at[half, rest], small_send.at[half])
        settle(reply.at[half, rest], reply_send.at[half])


def body(exciting, incident, pillar_type, type_matrix, near_coupling, screening, coupling_gain):
    rows, _, coef, width_x = exciting.shape
    groups = lax.axis_size("gx")
    parts = lax.axis_size("gy")
    used = OUTER * coef // parts
    slots = groups // 2
    dims = (rows, coef, width_x, used, slots, type_matrix.shape[0])
    twiddle, forward, inverse, phase = tables(width_x, coef, parts, slots, used)


    args = (
        exciting.transpose(0, 2, 1, 3),
        incident.transpose(0, 2, 1, 3),
        pillar_type,
        type_matrix.transpose(0, 2, 1, 3),
        near_coupling.transpose(2, 0, 1),
        screening.reshape(1, coef),
        coupling_gain,
        twiddle,
        forward,
        inverse,
        phase,
    )
    count = type_matrix.shape[0]
    halves = slots // SUB
    big = pltpu.VMEM((parts, rows, halves, 2, SUB, LANES), F32)
    line = pltpu.VMEM((parts, rows, 2, SUB, LANES), F32)
    small = pltpu.VMEM((halves, groups, 1, LANES), F32)
    dma = pltpu.SemaphoreType.DMA
    result = pl.pallas_call(
        functools.partial(fused, dims, groups, parts),
        out_shape=jax.ShapeDtypeStruct((rows, coef, 2, width_x), F32),
        in_specs=[pl.BlockSpec(memory_space=pltpu.VMEM)] * len(args),
        out_specs=pl.BlockSpec(memory_space=pltpu.VMEM),
        scratch_shapes=[
            pltpu.VMEM((count, 2 * GROUP, 6 * GROUP), F32),
            pltpu.VMEM((count * 2 * GROUP, 6 * GROUP), BF16),
            pltpu.VMEM((OUTER, 2, GROUP, LANES), F32),
            pltpu.VMEM((OUTER, GROUP, 2 * LANES), F32),
            big,
            pltpu.VMEM((parts + 2, rows, halves, 2, SUB, LANES), F32),
            small,
            small,
            small,
            small,
            pltpu.VMEM((2, 2, SUB, LANES), F32),
            pltpu.VMEM((5, 2, slots, LANES), F32),
            pltpu.VMEM((4, slots, LANES), F32),
            line,
            line,
            big,
            big,
            dma((rows, halves)),
            dma((rows, halves)),
            dma((halves,)),
            dma((halves,)),
            dma((halves,)),
            dma((halves,)),
            dma((2,)),
            dma((2,)),
            dma((rows, halves)),
            dma((rows, halves)),
        ],
        compiler_params=pltpu.CompilerParams(
            vmem_limit_bytes=VMEM_LIMIT, collective_id=0, has_side_effects=True
        ),
    )(*args)
    return result.transpose(0, 2, 1, 3)


def solution(mesh):
    placed = (
        P(("gx", "gy"), None, None, None),
        P(("gx", "gy"), None, None, None),
        P(("gx", "gy"), None),
        P(),
        P(),
        P(),
        P(),
    )
    return jax.shard_map(
        body,
        mesh=mesh,
        in_specs=placed,
        out_specs=P(("gx", "gy"), None, None, None),
        check_vma=False,
    )
```
